32 devices in a mesh: fsdp: 8 (over z, y), rep: 4 (over x, core).
Axes of the slice: x: 2, y: 2, z: 4, core: 2. Of those that a mesh axis runs over, the one named last changes fastest.
Arguments:
- tokens: bfloat16 [4, 8192, 1024], P('rep', 'fsdp'), may hold values from -6 to 6
- segment_ids: int32 [4, 8192], P('rep', 'fsdp'), may hold values from 0 to 255, as said below
- cotangent: bfloat16 [4, 8192, 1024], P('rep', 'fsdp'), may hold values from -6 to 6
- w_query: float32 [1024, 1024], P(('fsdp', 'rep')), may hold values from -0.1875 to 0.1875
- b_query: float32 [1024], P(('fsdp', 'rep')), may hold values from -1.75 to 1.75
- w_key: float32 [1024, 1024], P(('fsdp', 'rep')), may hold values from -0.1875 to 0.1875
- w_value: float32 [1024, 1024], P(('fsdp', 'rep')), may hold values from -0.1875 to 0.1875
- b_value: float32 [1024], P(('fsdp', 'rep')), may hold values from -3 to 3
- w_out: float32 [1024, 1024], P(('fsdp', 'rep')), may hold values from -0.75 to 0.75
- b_out: float32 [1024], P(('fsdp', 'rep')), may hold values from -3 to 3
- gain_attn: float32 [1024], P(('fsdp', 'rep')), may hold values from 0.5 to 1.5
- shift_attn: float32 [1024], P(('fsdp', 'rep')), may hold values from -3 to 3
- w_up: float32 [1024, 4096], P(('fsdp', 'rep')), may hold values from -0.1875 to 0.1875
- b_up: float32 [4096], P(('fsdp', 'rep')), may hold values from -3 to 3
- w_down: float32 [4096, 1024], P(('fsdp', 'rep')), may hold values from -0.09375 to 0.09375
- b_down: float32 [1024], P(('fsdp', 'rep')), may hold values from -3 to 3
- gain_ffn: float32 [1024], P(('fsdp', 'rep')), may hold values from 0.5 to 1.5
- shift_ffn: float32 [1024], P(('fsdp', 'rep')), may hold values from -3 to 3
Outputs:
- encoder_output: bfloat16 [4, 8192, 1024], P('rep', 'fsdp')
- layer_input_gradient: bfloat16 [4, 8192, 1024], P('rep', 'fsdp')
- grad_w_query: float32 [1024, 1024], P(('fsdp', 'rep'))
- grad_b_query: float32 [1024], P(('fsdp', 'rep'))
- grad_w_key: float32 [1024, 1024], P(('fsdp', 'rep'))
- grad_w_value: float32 [1024, 1024], P(('fsdp', 'rep'))
- grad_b_value: float32 [1024], P(('fsdp', 'rep'))
- grad_w_out: float32 [1024, 1024], P(('fsdp', 'rep'))
- grad_b_out: float32 [1024], P(('fsdp', 'rep'))
- grad_gain_attn: float32 [1024], P(('fsdp', 'rep'))
- grad_shift_attn: float32 [1024], P(('fsdp', 'rep'))
- grad_w_up: float32 [1024, 4096], P(('fsdp', 'rep'))
- grad_b_up: float32 [4096], P(('fsdp', 'rep'))
- grad_w_down: float32 [4096, 1024], P(('fsdp', 'rep'))
- grad_b_down: float32 [1024], P(('fsdp', 'rep'))
- grad_gain_ffn: float32 [1024], P(('fsdp', 'rep'))
- grad_shift_ffn: float32 [1024], P(('fsdp', 'rep'))
The draws below stay inside these ranges and needn't reach their ends.
Inputs may be any that keep to these rules, and one draw needn't show every extreme that they name: `segment_ids`: within each sequence of 1024 tokens the ids start at 0 and never fall; they stay below 256.
All inputs are finite; a program needn't handle non-finite values.
Results may differ from the reference program's by a relative error of at most 0.013.
The reference program's roundings to bfloat16 on the way count: a program that leaves them out, or rounds other values in their place, can miss the bound.
Values may be sent and summed in bfloat16 or wider, within the bound.
No kernel may reach another device: no remote copies, remote signals or barrier semaphores. Data moves between devices by JAX's collectives and lax.ppermute only.
A program may use at most 256 MiB of HBM per device.

```python
import math
import jax
import jax.numpy as jnp
from jax import lax

MODEL_WIDTH = 1024
HEADS = 16
HEAD_DIM = 64
FF = 4096
PACKED_TOKENS = 1024
BATCH_ROWS = 4
ROW_TOKENS = 8192


def draw_segment_ids(key, part):
    sequence_total = BATCH_ROWS * ROW_TOKENS // PACKED_TOKENS
    picked = jax.random.randint(jax.random.fold_in(key, 11), (sequence_total, 1), 0, 5)
    spacing = jnp.int32(2) ** (1 + 2 * picked)
    raw = jax.random.randint(jax.random.fold_in(key, 12), (sequence_total, PACKED_TOKENS), 0, 1 << 20)
    places = lax_iota(PACKED_TOKENS)
    flags = jnp.where((raw % spacing == 0) & (places[None, :] > 0), 1, 0).astype(jnp.int32)
    segment_labels = jnp.minimum(jnp.cumsum(flags, axis=1), 255)
    return segment_labels.reshape(BATCH_ROWS, ROW_TOKENS).astype(jnp.int32)


def lax_iota(length):
    return jnp.arange(length, dtype=jnp.int32)


def level_of(own_key, extent, shards, low, largest):
    def one(position, blocks):
        heights = jax.random.uniform(jax.random.fold_in(jax.random.fold_in(own_key, 6), position), (blocks,), jnp.float32, low / len(shards), largest / len(shards))
        return jnp.repeat(jnp.exp(heights), extent[position] // blocks).reshape((-1,) + (1,) * (len(extent) - position - 1))

    level = one(*shards[0])
    for cut in shards[1:]:
        level = level * one(*cut)
    return level


def bell_draw(key, extent, scale, bound, pieces=(), kind=jnp.bfloat16):
    result = jax.random.normal(key, extent, jnp.float32) * scale
    if len(pieces) > 0:
        result = level_of(key, extent, pieces, -0.22, 0.18) * result
    return jnp.clip(result, min=-bound, max=bound).astype(kind)


def setup_inputs(seed: int = 0) -> dict:
    key_list = jax.random.split(jax.random.key(seed), 19)
    return {
        "tokens": bell_draw(key_list[0], (BATCH_ROWS, ROW_TOKENS, MODEL_WIDTH), 1.0, 6.0, ((0, 4), (1, 8))),
        "segment_ids": draw_segment_ids(jax.random.fold_in(key_list[18], 71), 0),
        "cotangent": bell_draw(key_list[2], (BATCH_ROWS, ROW_TOKENS, MODEL_WIDTH), 1.0, 6.0, ((0, 4), (1, 8))),
        "w_query": bell_draw(key_list[3], (MODEL_WIDTH, MODEL_WIDTH), MODEL_WIDTH ** -0.5, 0.1875, ((0, 32),), jnp.float32),
        "b_query": bell_draw(key_list[4], (MODEL_WIDTH,), 0.3, 1.75, ((0, 32),), jnp.float32),
        "w_key": bell_draw(key_list[5], (MODEL_WIDTH, MODEL_WIDTH), MODEL_WIDTH ** -0.5, 0.1875, ((0, 32),), jnp.float32),
        "w_value": bell_draw(key_list[6], (MODEL_WIDTH, MODEL_WIDTH), MODEL_WIDTH ** -0.5, 0.1875, ((0, 32),), jnp.float32),
        "b_value": bell_draw(key_list[7], (MODEL_WIDTH,), 0.5, 3.0, ((0, 32),), jnp.float32),
        "w_out": bell_draw(key_list[8], (MODEL_WIDTH, MODEL_WIDTH), (MODEL_WIDTH // 16) ** -0.5, 0.75, ((0, 32),), jnp.float32),
        "b_out": bell_draw(key_list[9], (MODEL_WIDTH,), 0.5, 3.0, ((0, 32),), jnp.float32),
        "gain_attn": jnp.clip(1.0 + 0.1 * jax.random.normal(key_list[10], (MODEL_WIDTH,), jnp.float32), 0.5, 1.5),
        "shift_attn": bell_draw(key_list[11], (MODEL_WIDTH,), 0.5, 3.0, ((0, 32),), jnp.float32),
        "w_up": bell_draw(key_list[12], (MODEL_WIDTH, FF), MODEL_WIDTH ** -0.5, 0.1875, ((0, 32),), jnp.float32),
        "b_up": bell_draw(key_list[13], (FF,), 0.5, 3.0, ((0, 32),), jnp.float32),
        "w_down": bell_draw(key_list[14], (FF, MODEL_WIDTH), FF ** -0.5, 0.09375, ((0, 32),), jnp.float32),
        "b_down": bell_draw(key_list[15], (MODEL_WIDTH,), 0.5, 3.0, ((0, 32),), jnp.float32),
        "gain_ffn": jnp.clip(1.0 + 0.1 * jax.random.normal(key_list[16], (MODEL_WIDTH,), jnp.float32), 0.5, 1.5),
        "shift_ffn": bell_draw(key_list[17], (MODEL_WIDTH,), 0.5, 3.0, ((0, 32),), jnp.float32),
    }


@jax.custom_vjp
def low(v):
    return lax.optimization_barrier(v.astype(jnp.bfloat16)).astype(jnp.float32)

@jax.custom_vjp
def low_back(v):
    return v

def low_keep(v):
    return (low(v), None)

def low_pass(kept, grad):
    return (grad,)

def back_keep(v):
    return (v, None)

def back_low(kept, grad):
    return (low(grad),)
low.defvjp(low_keep, low_pass)
low_back.defvjp(back_keep, back_low)

def layer_norm(hidden, gain, shift):
    mean = lax.optimization_barrier(jnp.mean(hidden, axis=-1, keepdims=True))
    centered = hidden - mean
    variance = lax.optimization_barrier(jnp.mean(centered * centered, axis=-1, keepdims=True))
    return centered * lax.rsqrt(variance + 1e-05) * gain + shift

def project(values, weight):
    return jnp.einsum('gtd,de->gte', values, weight, precision=lax.Precision.HIGHEST)

def encoder(inputs, segments, params):
    w_query, b_query, w_key, w_value, b_value, w_out, b_out, gain_attn, shift_attn, w_up, b_up, w_down, b_down, gain_ffn, shift_ffn = params
    count, length, width = inputs.shape
    queries = low(low_back(project(inputs, w_query) + b_query))
    keys = low(low_back(project(inputs, w_key)))
    values = low(low_back(project(inputs, w_value) + b_value))

    def heads(v):
        return v.reshape(count, length, HEADS, HEAD_DIM)
    scores = jnp.einsum('gqhd,gkhd->ghqk', heads(queries), heads(keys), precision=lax.Precision.HIGHEST)
    scores = low_back(scores * 0.125)
    allowed = (segments[:, :, None] == segments[:, None, :])[:, None]
    scores = jnp.where(allowed, scores, -1e+30)
    probs = low(jax.nn.softmax(scores, axis=-1))
    context = jnp.einsum('ghqk,gkhd->gqhd', probs, heads(values), precision=lax.Precision.HIGHEST)
    context = low(low_back(context.reshape(count, length, width)))
    attended = low_back(project(context, w_out) + b_out)
    first = layer_norm(inputs + attended, gain_attn, shift_attn)
    pre = low_back(project(low(first), w_up) + b_up)
    hidden = low(jax.nn.gelu(pre, approximate=False))
    branch = low_back(project(hidden, w_down) + b_down)
    return layer_norm(first + branch, gain_ffn, shift_ffn)

def reference(tokens, segment_ids, cotangent, w_query, b_query, w_key, w_value, b_value, w_out, b_out, gain_attn, shift_attn, w_up, b_up, w_down, b_down, gain_ffn, shift_ffn):
    masters = (w_query, b_query, w_key, w_value, b_value, w_out, b_out, gain_attn, shift_attn, w_up, b_up, w_down, b_down, gain_ffn, shift_ffn)
    sequence_total = BATCH_ROWS * ROW_TOKENS // PACKED_TOKENS
    group = math.gcd(sequence_total, max(1, 4096 // PACKED_TOKENS))
    inputs = tokens.astype(jnp.float32).reshape(sequence_total // group, group, PACKED_TOKENS, MODEL_WIDTH)
    segments = segment_ids.reshape(sequence_total // group, group, PACKED_TOKENS)
    incoming = cotangent.astype(jnp.float32).reshape(sequence_total // group, group, PACKED_TOKENS, MODEL_WIDTH)
    checked = jax.checkpoint(encoder)

    def whole(inputs, masters):
        rounded = tuple((low(p) for p in masters))

        def step(carry, item):
            return (carry, checked(item[0], item[1], rounded))
        _, final_outcome = lax.scan(step, jnp.zeros((), jnp.float32), (inputs, segments))
        return final_outcome
    final_outcome, pull = jax.vjp(whole, inputs, masters)
    input_gradients, grad_params = pull(incoming)
    encoder_output = final_outcome.reshape(BATCH_ROWS, ROW_TOKENS, MODEL_WIDTH).astype(jnp.bfloat16)
    layer_input_gradient = input_gradients.reshape(BATCH_ROWS, ROW_TOKENS, MODEL_WIDTH).astype(jnp.bfloat16)
    return (encoder_output, layer_input_gradient, grad_params[0], grad_params[1], grad_params[2], grad_params[3], grad_params[4], grad_params[5], grad_params[6], grad_params[7], grad_params[8], grad_params[9], grad_params[10], grad_params[11], grad_params[12], grad_params[13], grad_params[14])
```

```python
from functools import partial

import jax
import jax.numpy as jnp
from jax import lax
from jax.experimental import pallas as pl
from jax.experimental.pallas import tpu as pltpu
from jax.sharding import PartitionSpec as P

HEAD_DIM = 64
PAIR = 128
TILE = 256
CHUNKS = 4
SCALE = 0.125
EPS = 1e-05
NEG = -1e30
AXES = ("fsdp", "rep")
BF = jnp.bfloat16
F32 = jnp.float32


def matmul(left, right):
    return jnp.dot(left, right, preferred_element_type=F32)


def contract_rows(left, right):
    return lax.dot_general(left, right, (((0,), (0,)), ((), ())), preferred_element_type=F32)


def contract_cols(left, right):
    return lax.dot_general(left, right, (((1,), (1,)), ((), ())), preferred_element_type=F32)


def normalize(hidden, gain, shift):
    mean = jnp.mean(hidden, axis=-1, keepdims=True)
    centered = hidden - mean
    inverse = lax.rsqrt(jnp.mean(centered * centered, axis=-1, keepdims=True) + EPS)
    normed = centered * inverse
    return (normed * gain + shift, normed, inverse)


def normalize_back(grad, normed, inverse, gain):
    scaled = grad * gain
    inner = scaled - jnp.mean(scaled, axis=-1, keepdims=True)
    inner = inner - normed * jnp.mean(scaled * normed, axis=-1, keepdims=True)
    return (inverse * inner, jnp.sum(grad * normed, axis=0), jnp.sum(grad, axis=0))


def fill_bias(seg_col, seg_row, bias):
    @pl.when(pl.program_id(0) == 0)
    def _():
        bias[...] = jnp.where(seg_col[...] == seg_row[...], 0.0, NEG)


def head_lanes(head):
    lane = lax.broadcasted_iota(jnp.int32, (TILE, PAIR), 1)
    return lane < HEAD_DIM if head == 0 else lane >= HEAD_DIM


def forward_kernel(seg_col, seg_row, q_ref, k_ref, v_ref, o_ref, lse_ref, bias, out_t):
    fill_bias(seg_col, seg_row, bias)
    keys = k_ref[...]
    values_t = v_ref[...].T
    for tile in range(q_ref.shape[0] // TILE):
        at = slice(tile * TILE, (tile + 1) * TILE)
        query = q_ref[at, :] * jnp.asarray(SCALE, BF)
        for head in range(2):
            mine = jnp.where(head_lanes(head), query, jnp.zeros_like(query))
            scores = contract_cols(keys, mine) + bias[:, at]
            top = jnp.max(scores, axis=0, keepdims=True)
            weights = jnp.exp(scores - top)
            total = jnp.sum(weights, axis=0, keepdims=True)
            probs = (weights * (1.0 / total)).astype(BF)
            rows = slice(head * HEAD_DIM, (head + 1) * HEAD_DIM)
            out_t[rows, at] = matmul(values_t[rows, :], probs)
            lse_ref[0, head : head + 1, at] = top + jnp.log(total)
    o_ref[...] = out_t[...].T.astype(BF)


def backward_kernel(
    seg_col, seg_row, q_ref, k_ref, v_ref, do_ref, lse_ref,
    dq_ref, dk_ref, dv_ref, bq_ref, bv_ref, bias, dq_t, dk_sum, dv_sum,
):
    fill_bias(seg_col, seg_row, bias)
    keys = k_ref[...]
    values = v_ref[...]
    keys_t = keys.T
    for tile in range(q_ref.shape[0] // TILE):
        at = slice(tile * TILE, (tile + 1) * TILE)
        query = q_ref[at, :]
        grad = do_ref[at, :]
        for head in range(2):
            lanes = head_lanes(head)
            query_h = jnp.where(lanes, query, jnp.zeros_like(query))
            grad_h = jnp.where(lanes, grad, jnp.zeros_like(grad))
            scores = contract_cols(keys, query_h * jnp.asarray(SCALE, BF)) + bias[:, at]
            probs = jnp.exp(scores - lse_ref[0, head : head + 1, at])
            grad_probs = contract_cols(values, grad_h)
            inner = jnp.sum(grad_probs * probs, axis=0, keepdims=True)
            grad_scores = (probs * (grad_probs - inner)).astype(BF)
            rows = slice(head * HEAD_DIM, (head + 1) * HEAD_DIM)
            dq_t[rows, at] = matmul(keys_t[rows, :], grad_scores)
            dk_part = matmul(grad_scores, query_h)
            dv_part = matmul(probs.astype(BF), grad_h)
            if tile == 0 and head == 0:
                dk_sum[...] = dk_part
                dv_sum[...] = dv_part
            else:
                dk_sum[...] += dk_part
                dv_sum[...] += dv_part
    dq = (dq_t[...].T * SCALE).astype(BF)
    dv = dv_sum[...].astype(BF)
    dq_ref[...] = dq
    dk_ref[...] = (dk_sum[...] * SCALE).astype(BF)
    dv_ref[...] = dv
    bq_ref[...] = jnp.sum(dq.astype(F32), axis=0, keepdims=True)
    bv_ref[...] = jnp.sum(dv.astype(F32), axis=0, keepdims=True)


def columns(tokens, first):
    return pl.BlockSpec((tokens, PAIR), lambda i: (0, first + i))


def segment_specs(tokens):
    return [pl.BlockSpec((tokens, 1), lambda i: (0, 0)), pl.BlockSpec((1, tokens), lambda i: (0, 0))]


PARAMS = pltpu.CompilerParams(dimension_semantics=("arbitrary",), vmem_limit_bytes=56 * 2**20)


def attend(segments, packed):
    tokens = packed.shape[0]
    width = packed.shape[1] // 3
    pairs = width // PAIR
    return pl.pallas_call(
        forward_kernel,
        grid=(pairs,),
        name="attend",
        in_specs=segment_specs(tokens) + [columns(tokens, part * pairs) for part in range(3)],
        out_specs=[columns(tokens, 0), pl.BlockSpec((1, 2, tokens), lambda i: (i, 0, 0))],
        out_shape=[
            jax.ShapeDtypeStruct((tokens, width), BF),
            jax.ShapeDtypeStruct((pairs, 2, tokens), F32),
        ],
        scratch_shapes=[pltpu.VMEM((tokens, tokens), F32), pltpu.VMEM((PAIR, tokens), F32)],
        compiler_params=PARAMS,
    )(segments.reshape(tokens, 1), segments.reshape(1, tokens), packed, packed, packed)


def attend_back(segments, packed, grad, logsum, chunk):
    tokens = packed.shape[0]
    width = packed.shape[1] // 3
    pairs = width // PAIR
    count = pairs // CHUNKS
    first = chunk * count
    row = pl.BlockSpec((1, PAIR), lambda i: (0, i))
    return pl.pallas_call(
        backward_kernel,
        grid=(count,),
        name="attend_back",
        in_specs=segment_specs(tokens)
        + [columns(tokens, part * pairs + first) for part in range(3)]
        + [columns(tokens, first), pl.BlockSpec((1, 2, tokens), lambda i: (first + i, 0, 0))],
        out_specs=[columns(tokens, 0)] * 3 + [row] * 2,
        out_shape=[jax.ShapeDtypeStruct((tokens, count * PAIR), BF)] * 3
        + [jax.ShapeDtypeStruct((1, count * PAIR), F32)] * 2,
        scratch_shapes=[
            pltpu.VMEM((tokens, tokens), F32),
            pltpu.VMEM((PAIR, tokens), F32),
            pltpu.VMEM((tokens, PAIR), F32),
            pltpu.VMEM((tokens, PAIR), F32),
        ],
        compiler_params=PARAMS,
    )(segments.reshape(tokens, 1), segments.reshape(1, tokens), packed, packed, packed, grad, logsum)


def swap(value, bit, devices):
    return lax.ppermute(value, AXES, [(i, i ^ (1 << bit)) for i in range(devices)])


def bit_orders(bits):
    rest = list(range(1, bits))
    starts = (0, (bits - 1) // 4, (bits - 1) // 2)
    return [[0] + rest[s:] + rest[:s] for s in starts]


def spans(width, parts):
    step = width // PAIR // parts * PAIR
    edges = [step * p for p in range(parts)] + [width]
    return list(zip(edges[:-1], edges[1:]))


def scatter_one(value, order, devices, kind):
    bits = devices.bit_length() - 1
    here = lax.axis_index(AXES)
    work = value.reshape((2,) * bits + (value.shape[0] // devices, value.shape[1]))
    left = list(range(bits))
    for bit in order:
        axis = left.index(bits - 1 - bit)
        own = (here >> bit) & 1
        keep = lax.dynamic_index_in_dim(work, own, axis, keepdims=False)
        send = lax.dynamic_index_in_dim(work, 1 - own, axis, keepdims=False).astype(kind)
        work = keep.astype(F32) + swap(send, bit, devices).astype(F32)
        left.pop(axis)
    return work


def scatter(value, devices, parts=3, kind=BF, turn=0):
    orders = bit_orders(devices.bit_length() - 1)
    done = [
        scatter_one(value[:, a:b], orders[(p + turn) % 3], devices, kind)
        for p, (a, b) in enumerate(spans(value.shape[1], parts))
    ]
    return jnp.concatenate(done, axis=1)


def gather_one(value, order, devices):
    bits = devices.bit_length() - 1
    here = lax.axis_index(AXES)
    work = value
    held = []
    for bit in order:
        name = bits - 1 - bit
        axis = sum(1 for h in held if h < name)
        own = (here >> bit) & 1
        got = swap(work, bit, devices)
        work = jnp.where(own == 0, jnp.stack([work, got], axis), jnp.stack([got, work], axis))
        held = sorted(held + [name])
    return work.reshape(devices * value.shape[0], value.shape[1])


def gather_pairs(value, devices, parts=3):
    orders = bit_orders(devices.bit_length() - 1)
    return [
        gather_one(value[:, a:b], orders[p][::-1], devices)
        for p, (a, b) in enumerate(spans(value.shape[1], parts))
    ]


def widen(vector):
    return vector.astype(F32)


def local(
    tokens, segment_ids, cotangent, w_query, b_query, w_key, w_value, b_value, w_out, b_out,
    gain_attn, shift_attn, w_up, b_up, w_down, b_down, gain_ffn, shift_ffn, devices,
):
    blocks, length, width = tokens.shape
    rows = tokens.reshape(blocks * length, width)
    own = w_query.shape[0]
    ratio = b_up.shape[0] // own
    vectors = [b_query, b_value, b_out, gain_attn, shift_attn, b_down, gain_ffn, shift_ffn]
    names = len(vectors)
    side = jnp.stack(vectors, axis=1)
    side = jnp.concatenate([side, b_up.reshape(own, ratio)], axis=1)
    side = jnp.pad(side, ((0, 0), (0, PAIR - names - ratio)))
    head = jnp.concatenate([side, w_query, w_key, w_value], axis=1).astype(BF)
    head = jnp.concatenate(gather_pairs(head, devices), axis=1)
    packed_full = head[:, PAIR:]
    query_bias, value_bias, out_bias, attn_gain, attn_shift, down_bias, ffn_gain, ffn_shift = [
        widen(head[:, i]) for i in range(names)
    ]
    up_bias = widen(head[:, names : names + ratio].reshape(-1))
    out_up = lax.all_gather(jnp.concatenate([w_out, w_up], axis=1).astype(BF), AXES, axis=0, tiled=True)
    down_full = lax.all_gather(w_down.astype(BF), AXES, axis=0, tiled=True)
    out_full, up_full = out_up[:, :width], out_up[:, width:]

    packed_bias = jnp.concatenate([query_bias, jnp.zeros_like(query_bias), value_bias])
    packed = (matmul(rows, packed_full) + packed_bias).astype(BF)
    segments = segment_ids.reshape(-1)
    context, logsums = attend(segments, packed)
    attended = matmul(context, out_full) + out_bias
    first, normed_one, inverse_one = normalize(rows.astype(F32) + attended, attn_gain, attn_shift)
    first_low = first.astype(BF)
    pre = matmul(first_low, up_full) + up_bias
    hidden = jax.nn.gelu(pre, approximate=False).astype(BF)
    branch = matmul(hidden, down_full) + down_bias
    output, normed_two, inverse_two = normalize(first + branch, ffn_gain, ffn_shift)
    encoder_output = output.astype(BF).reshape(tokens.shape)

    incoming = cotangent.reshape(blocks * length, width).astype(F32)
    grad_two, ffn_gain_grad, ffn_shift_grad = normalize_back(incoming, normed_two, inverse_two, ffn_gain)
    grad_branch = grad_two.astype(BF)
    down_grad = scatter(contract_rows(hidden, grad_branch).astype(BF), devices)
    down_bias_grad = jnp.sum(grad_branch.astype(F32), axis=0)
    grad_hidden = contract_cols(grad_branch, down_full)
    _, gelu_pull = jax.vjp(partial(jax.nn.gelu, approximate=False), pre)
    grad_pre = gelu_pull(grad_hidden)[0].astype(BF)
    up_grad = scatter(contract_rows(first_low, grad_pre).astype(BF), devices)
    up_bias_grad = jnp.sum(grad_pre.astype(F32), axis=0)
    grad_first = grad_two + contract_cols(grad_pre, up_full)
    grad_one, attn_gain_grad, attn_shift_grad = normalize_back(grad_first, normed_one, inverse_one, attn_gain)
    grad_attended = grad_one.astype(BF)
    out_grad = scatter(contract_rows(context, grad_attended).astype(BF), devices)
    out_bias_grad = jnp.sum(grad_attended.astype(F32), axis=0)
    grad_context = contract_cols(grad_attended, out_full).astype(BF)

    pieces, shares = [], []
    for chunk in range(CHUNKS):
        piece = attend_back(segments, packed, grad_context, logsums, chunk)
        pieces.append(piece)
        grads = jnp.concatenate([contract_rows(rows, part).astype(BF) for part in piece[:3]], axis=1)
        shares.append(scatter(grads, devices))
    joined = [jnp.concatenate([piece[part] for piece in pieces], axis=1) for part in range(5)]
    total = jnp.concatenate(joined[:3], axis=1)
    total_input = grad_one + contract_cols(total, packed_full)
    layer_input_gradient = total_input.astype(BF).reshape(tokens.shape)

    step = width // CHUNKS
    query_grad, key_grad, value_grad = [
        jnp.concatenate([share[:, part * step : (part + 1) * step] for share in shares], axis=1)
        for part in range(3)
    ]
    vector_grads = [
        joined[3][0], joined[4][0], out_bias_grad, attn_gain_grad, attn_shift_grad,
        down_bias_grad, ffn_gain_grad, ffn_shift_grad,
    ]
    side_grad = jnp.concatenate(
        [v.reshape(devices, own) for v in vector_grads] + [up_bias_grad.reshape(devices, own * ratio)],
        axis=1,
    )
    side_grad = scatter(side_grad, devices, parts=1, kind=F32)[0]
    parts = [side_grad[i * own : (i + 1) * own] for i in range(names)]
    up_bias_share = side_grad[names * own :]
    return (
        encoder_output, layer_input_gradient, query_grad, parts[0], key_grad, value_grad, parts[1],
        out_grad, parts[2], parts[3], parts[4], up_grad, up_bias_share, down_grad, parts[5],
        parts[6], parts[7],
    )


def solution(mesh):
    devices = mesh.shape["fsdp"] * mesh.shape["rep"]
    act, ids = P("rep", "fsdp", None), P("rep", "fsdp")
    mat, vec = P(AXES, None), P(AXES)
    return jax.shard_map(
        partial(local, devices=devices),
        mesh=mesh,
        in_specs=(
            act, ids, act, mat, vec, mat, mat, vec, mat, vec, vec, vec, mat, vec, mat, vec, vec, vec,
        ),
        out_specs=(act, act, mat, vec, mat, mat, vec, mat, vec, vec, vec, mat, vec, mat, vec, vec, vec),
        check_vma=False,
    )
```

```python
from functools import partial

import jax
import jax.numpy as jnp
from jax import lax
from jax.experimental import pallas as pl
from jax.experimental.pallas import tpu as pltpu
from jax.sharding import PartitionSpec as P


HEAD_DIM = 64
PAIR = 128
TILE = 256
CHUNKS = 4
SCALE = 0.125
EPS = 1e-05
NEG = -1e30
AXES = ("fsdp", "rep")
BF = jnp.bfloat16
F32 = jnp.float32


def matmul(left, right):
    return jnp.dot(left, right, preferred_element_type=F32)


def contract_rows(left, right):
    return lax.dot_general(left, right, (((0,), (0,)), ((), ())), preferred_element_type=F32)


def contract_cols(left, right):
    return lax.dot_general(left, right, (((1,), (1,)), ((), ())), preferred_element_type=F32)


def normalize(hidden, gain, shift):
    mean = jnp.mean(hidden, axis=-1, keepdims=True)
    centered = hidden - mean
    inverse = lax.rsqrt(jnp.mean(centered * centered, axis=-1, keepdims=True) + EPS)
    normed = centered * inverse
    return (normed * gain + shift, normed, inverse)


def normalize_back(grad, normed, inverse, gain):
    scaled = grad * gain
    inner = scaled - jnp.mean(scaled, axis=-1, keepdims=True)
    inner = inner - normed * jnp.mean(scaled * normed, axis=-1, keepdims=True)
    return (inverse * inner, jnp.sum(grad * normed, axis=0), jnp.sum(grad, axis=0))


def fill_bias(seg_col, seg_row, bias):
    @pl.when(pl.program_id(0) == 0)
    def _():
        bias[...] = jnp.where(seg_col[...] == seg_row[...], 0.0, NEG)


def head_lanes(head):
    lane = lax.broadcasted_iota(jnp.int32, (TILE, PAIR), 1)
    return lane < HEAD_DIM if head == 0 else lane >= HEAD_DIM


def forward_kernel(seg_col, seg_row, q_ref, k_ref, v_ref, o_ref, lse_ref, bias, out_t):
    fill_bias(seg_col, seg_row, bias)
    keys = k_ref[...]
    values_t = v_ref[...].T
    for tile in range(q_ref.shape[0] // TILE):
        at = slice(tile * TILE, (tile + 1) * TILE)
        query = q_ref[at, :] * jnp.asarray(SCALE, BF)
        for head in range(2):
            mine = jnp.where(head_lanes(head), query, jnp.zeros_like(query))
            scores = contract_cols(keys, mine) + bias[:, at]
            top = jnp.max(scores, axis=0, keepdims=True)
            weights = jnp.exp(scores - top)
            total = jnp.sum(weights, axis=0, keepdims=True)
            probs = (weights * (1.0 / total)).astype(BF)
            rows = slice(head * HEAD_DIM, (head + 1) * HEAD_DIM)
            out_t[rows, at] = matmul(values_t[rows, :], probs)
            lse_ref[0, head : head + 1, at] = top + jnp.log(total)
    o_ref[...] = out_t[...].T.astype(BF)


def backward_kernel(
    seg_col, seg_row, q_ref, k_ref, v_ref, do_ref, lse_ref,
    dq_ref, dk_ref, dv_ref, bq_ref, bv_ref, bias, dq_t, dk_sum, dv_sum,
):
    fill_bias(seg_col, seg_row, bias)
    keys = k_ref[...]
    values = v_ref[...]
    keys_t = keys.T
    for tile in range(q_ref.shape[0] // TILE):
        at = slice(tile * TILE, (tile + 1) * TILE)
        query = q_ref[at, :]
        grad = do_ref[at, :]
        for head in range(2):
            lanes = head_lanes(head)
            query_h = jnp.where(lanes, query, jnp.zeros_like(query))
            grad_h = jnp.where(lanes, grad, jnp.zeros_like(grad))
            scores = contract_cols(keys, query_h * jnp.asarray(SCALE, BF)) + bias[:, at]
            probs = jnp.exp(scores - lse_ref[0, head : head + 1, at])
            grad_probs = contract_cols(values, grad_h)
            inner = jnp.sum(grad_probs * probs, axis=0, keepdims=True)
            grad_scores = (probs * (grad_probs - inner)).astype(BF)
            rows = slice(head * HEAD_DIM, (head + 1) * HEAD_DIM)
            dq_t[rows, at] = matmul(keys_t[rows, :], grad_scores)
            dk_part = matmul(grad_scores, query_h)
            dv_part = matmul(probs.astype(BF), grad_h)
            if tile == 0 and head == 0:
                dk_sum[...] = dk_part
                dv_sum[...] = dv_part
            else:
                dk_sum[...] += dk_part
                dv_sum[...] += dv_part
    dq = (dq_t[...].T * SCALE).astype(BF)
    dv = dv_sum[...].astype(BF)
    dq_ref[...] = dq
    dk_ref[...] = (dk_sum[...] * SCALE).astype(BF)
    dv_ref[...] = dv
    bq_ref[...] = jnp.sum(dq.astype(F32), axis=0, keepdims=True)
    bv_ref[...] = jnp.sum(dv.astype(F32), axis=0, keepdims=True)


def columns(tokens, first):
    return pl.BlockSpec((tokens, PAIR), lambda i: (0, first + i))


def segment_specs(tokens):
    return [pl.BlockSpec((tokens, 1), lambda i: (0, 0)), pl.BlockSpec((1, tokens), lambda i: (0, 0))]


PARAMS = pltpu.CompilerParams(dimension_semantics=("arbitrary",), vmem_limit_bytes=56 * 2**20)


def attend(segments, packed):
    tokens = packed.shape[0]
    width = packed.shape[1] // 3
    pairs = width // PAIR
    return pl.pallas_call(
        forward_kernel,
        grid=(pairs,),
        name="attend",
        in_specs=segment_specs(tokens) + [columns(tokens, part * pairs) for part in range(3)],
        out_specs=[columns(tokens, 0), pl.BlockSpec((1, 2, tokens), lambda i: (i, 0, 0))],
        out_shape=[
            jax.ShapeDtypeStruct((tokens, width), BF),
            jax.ShapeDtypeStruct((pairs, 2, tokens), F32),
        ],
        scratch_shapes=[pltpu.VMEM((tokens, tokens), F32), pltpu.VMEM((PAIR, tokens), F32)],
        compiler_params=PARAMS,
    )(segments.reshape(tokens, 1), segments.reshape(1, tokens), packed, packed, packed)


def attend_back(segments, packed, grad, logsum, chunk):
    tokens = packed.shape[0]
    width = packed.shape[1] // 3
    pairs = width // PAIR
    count = pairs // CHUNKS
    first = chunk * count
    row = pl.BlockSpec((1, PAIR), lambda i: (0, i))
    return pl.pallas_call(
        backward_kernel,
        grid=(count,),
        name="attend_back",
        in_specs=segment_specs(tokens)
        + [columns(tokens, part * pairs + first) for part in range(3)]
        + [columns(tokens, first), pl.BlockSpec((1, 2, tokens), lambda i: (first + i, 0, 0))],
        out_specs=[columns(tokens, 0)] * 3 + [row] * 2,
        out_shape=[jax.ShapeDtypeStruct((tokens, count * PAIR), BF)] * 3
        + [jax.ShapeDtypeStruct((1, count * PAIR), F32)] * 2,
        scratch_shapes=[
            pltpu.VMEM((tokens, tokens), F32),
            pltpu.VMEM((PAIR, tokens), F32),
            pltpu.VMEM((tokens, PAIR), F32),
            pltpu.VMEM((tokens, PAIR), F32),
        ],
        compiler_params=PARAMS,
    )(segments.reshape(tokens, 1), segments.reshape(1, tokens), packed, packed, packed, grad, logsum)


def swap(value, bit, devices):
    return lax.ppermute(value, AXES, [(i, i ^ (1 << bit)) for i in range(devices)])


def bit_orders(bits):
    rest = list(range(1, bits))
    starts = (0, (bits - 1) // 4, (bits - 1) // 2)
    return [[0] + rest[s:] + rest[:s] for s in starts]


def spans(width, parts):
    step = width // PAIR // parts * PAIR
    edges = [step * p for p in range(parts)] + [width]
    return list(zip(edges[:-1], edges[1:]))


class Chain:
    def __init__(self, value, order, devices, kind=BF):
        self.devices, self.kind, self.order = devices, kind, list(order)
        self.left = list(range(devices.bit_length() - 1))
        self.halve(value.reshape((2,) * len(self.left) + (value.shape[0] // devices, value.shape[1])))
        self.got = None

    def halve(self, work):
        bit = self.order[0]
        axis = self.left.index(len(range(self.devices.bit_length() - 1)) - 1 - bit)
        own = (lax.axis_index(AXES) >> bit) & 1
        self.keep = lax.dynamic_index_in_dim(work, own, axis, keepdims=False)
        self.send = lax.dynamic_index_in_dim(work, 1 - own, axis, keepdims=False).astype(self.kind)
        self.left.pop(axis)

    def begin(self):
        self.got = swap(self.send, self.order.pop(0), self.devices)

    def finish(self):
        total = self.keep.astype(F32) + self.got.astype(F32)
        self.got = None
        if self.order:
            self.halve(total)
        else:
            self.keep, self.send = total, None

    @property
    def over(self):
        return self.send is None


def tick(chains, value):
    active = [c for c in chains if not c.over]
    for c in active:
        if c.got is not None:
            c.finish()
    held = lax.optimization_barrier((value, [(c.keep, c.send) for c in active]))
    for c, (keep, send) in zip(active, held[1]):
        c.keep, c.send = keep, send
        if not c.over:
            c.begin()
    return held[0]


def chains_of(value, devices, parts=3, turn=0, kind=BF):
    orders = bit_orders(devices.bit_length() - 1)
    return [
        Chain(value[:, a:b], orders[(p + turn) % 3], devices, kind)
        for p, (a, b) in enumerate(spans(value.shape[1], parts))
    ]


def result(chains):
    return jnp.concatenate([c.keep for c in chains], axis=1)


def gather_pairs(value, devices, later, parts=3):
    bits = devices.bit_length() - 1
    here = lax.axis_index(AXES)
    orders = [order[::-1] for order in bit_orders(bits)]
    work = [value[:, a:b] for a, b in spans(value.shape[1], parts)]
    held = [[] for _ in range(parts)]
    for step in range(bits):
        for p in range(parts):
            bit = orders[p][step]
            name = bits - 1 - bit
            axis = sum(1 for h in held[p] if h < name)
            own = (here >> bit) & 1
            mine, got = work[p], swap(work[p], bit, devices)
            work[p] = jnp.where(own == 0, jnp.stack([mine, got], axis), jnp.stack([got, mine], axis))
            held[p] = sorted(held[p] + [name])
        if step == bits - 3:
            work, later = lax.optimization_barrier((work, later))
    return [w.reshape(devices * value.shape[0], w.shape[-1]) for w in work], later


def widen(vector):
    return vector.astype(F32)


def local(
    tokens, segment_ids, cotangent, w_query, b_query, w_key, w_value, b_value, w_out, b_out,
    gain_attn, shift_attn, w_up, b_up, w_down, b_down, gain_ffn, shift_ffn, devices,
):
    blocks, length, width = tokens.shape
    rows = tokens.reshape(blocks * length, width)
    own = w_query.shape[0]
    ratio = b_up.shape[0] // own
    vectors = [b_query, b_value, b_out, gain_attn, shift_attn, b_down, gain_ffn, shift_ffn]
    names = len(vectors)
    side = jnp.stack(vectors, axis=1)
    side = jnp.concatenate([side, b_up.reshape(own, ratio)], axis=1)
    side = jnp.pad(side, ((0, 0), (0, PAIR - names - ratio)))
    head = jnp.concatenate([side, w_query, w_key, w_value], axis=1).astype(BF)
    later = (jnp.concatenate([w_out, w_up], axis=1).astype(BF), w_down.astype(BF))
    head, later = gather_pairs(head, devices, later)
    head = jnp.concatenate(head, axis=1)
    packed_full = head[:, PAIR:]
    query_bias, value_bias, out_bias, attn_gain, attn_shift, down_bias, ffn_gain, ffn_shift = [
        widen(head[:, i]) for i in range(names)
    ]
    up_bias = widen(head[:, names : names + ratio].reshape(-1))
    out_up = lax.all_gather(later[0], AXES, axis=0, tiled=True)
    down_full = lax.all_gather(later[1], AXES, axis=0, tiled=True)
    out_full, up_full = out_up[:, :width], out_up[:, width:]

    packed_bias = jnp.concatenate([query_bias, jnp.zeros_like(query_bias), value_bias])
    packed = (matmul(rows, packed_full) + packed_bias).astype(BF)
    segments = segment_ids.reshape(-1)
    context, logsums = attend(segments, packed)
    attended = matmul(context, out_full) + out_bias
    first, normed_one, inverse_one = normalize(rows.astype(F32) + attended, attn_gain, attn_shift)
    first_low = first.astype(BF)
    pre = matmul(first_low, up_full) + up_bias
    hidden = jax.nn.gelu(pre, approximate=False).astype(BF)
    branch = matmul(hidden, down_full) + down_bias
    output, normed_two, inverse_two = normalize(first + branch, ffn_gain, ffn_shift)
    encoder_output = output.astype(BF).reshape(tokens.shape)

    incoming = cotangent.reshape(blocks * length, width).astype(F32)
    grad_two, ffn_gain_grad, ffn_shift_grad = normalize_back(incoming, normed_two, inverse_two, ffn_gain)
    grad_branch = grad_two.astype(BF)
    down = chains_of(contract_rows(hidden, grad_branch).astype(BF), devices)
    down_bias_grad = jnp.sum(grad_branch.astype(F32), axis=0)
    running = list(down)
    grad_branch = tick(running, grad_branch)
    grad_hidden = contract_cols(grad_branch, down_full)
    _, gelu_pull = jax.vjp(partial(jax.nn.gelu, approximate=False), pre)
    grad_pre = gelu_pull(grad_hidden)[0].astype(BF)
    up_bias_grad = jnp.sum(grad_pre.astype(F32), axis=0)
    grad_pre = tick(running, grad_pre)
    up_product = contract_rows(first_low, grad_pre).astype(BF)
    up = chains_of(up_product, devices, turn=1)
    running += up
    grad_pre = tick(running, grad_pre)
    grad_first = grad_two + contract_cols(grad_pre, up_full)
    grad_one, attn_gain_grad, attn_shift_grad = normalize_back(grad_first, normed_one, inverse_one, attn_gain)
    grad_attended = grad_one.astype(BF)
    out_bias_grad = jnp.sum(grad_attended.astype(F32), axis=0)
    grad_attended = tick(running, grad_attended)
    out_product = contract_rows(context, grad_attended).astype(BF)
    out = chains_of(out_product, devices, parts=1, turn=2)
    grad_context = contract_cols(grad_attended, out_full).astype(BF)
    running += out

    pieces, shares = [], []
    for chunk in range(CHUNKS):
        grad_context = tick(running, grad_context)
        piece = attend_back(segments, packed, grad_context, logsums, chunk)
        if chunk + 1 < CHUNKS:
            grad_context, piece = lax.optimization_barrier((grad_context, piece))
        pieces.append(piece)
        grads = jnp.concatenate([contract_rows(rows, part).astype(BF) for part in piece[:3]], axis=1)
        shares.append(chains_of(grads, devices, parts=1, turn=chunk))
        running += shares[-1]
    joined = [jnp.concatenate([piece[part] for piece in pieces], axis=1) for part in range(5)]
    vector_grads = [
        joined[3][0], joined[4][0], out_bias_grad, attn_gain_grad, attn_shift_grad,
        down_bias_grad, ffn_gain_grad, ffn_shift_grad,
    ]
    side_grad = jnp.concatenate(
        [v.reshape(devices, own) for v in vector_grads] + [up_bias_grad.reshape(devices, own * ratio)],
        axis=1,
    )
    side = chains_of(side_grad, devices, parts=1, kind=F32)
    running += side
    total = tick(running, jnp.concatenate(joined[:3], axis=1))
    total_input = grad_one + contract_cols(total, packed_full)
    layer_input_gradient = total_input.astype(BF).reshape(tokens.shape)
    while not all(c.over for c in running):
        tick(running, ())

    down_grad, up_grad, out_grad = result(down), result(up), result(out)
    shares = [result(share) for share in shares]
    step = width // CHUNKS
    query_grad, key_grad, value_grad = [
        jnp.concatenate([share[:, part * step : (part + 1) * step] for share in shares], axis=1)
        for part in range(3)
    ]
    side_grad = result(side)[0]
    parts = [side_grad[i * own : (i + 1) * own] for i in range(names)]
    up_bias_share = side_grad[names * own :]
    return (
        encoder_output, layer_input_gradient, query_grad, parts[0], key_grad, value_grad, parts[1],
        out_grad, parts[2], parts[3], parts[4], up_grad, up_bias_share, down_grad, parts[5],
        parts[6], parts[7],
    )


def solution(mesh):
    devices = mesh.shape["fsdp"] * mesh.shape["rep"]
    act, ids = P("rep", "fsdp", None), P("rep", "fsdp")
    mat, vec = P(AXES, None), P(AXES)
    return jax.shard_map(
        partial(local, devices=devices),
        mesh=mesh,
        in_specs=(
            act, ids, act, mat, vec, mat, mat, vec, mat, vec, vec, vec, mat, vec, mat, vec, vec, vec,
        ),
        out_specs=(act, act, mat, vec, mat, mat, vec, mat, vec, vec, vec, mat, vec, mat, vec, vec, vec),
        check_vma=False,
    )
```

```python
from functools import partial

import jax
import jax.numpy as jnp
from jax import lax
from jax.experimental import pallas as pl
from jax.experimental.pallas import tpu as pltpu
from jax.sharding import PartitionSpec as P


HEAD_DIM = 64
PAIR = 128
TILE = 256
CHUNKS = 4
SCALE = 0.125
EPS = 1e-05
NEG = -1e30
BELL = (2.0 * 3.141592653589793) ** -0.5
AXES = ("fsdp", "rep")
BF = jnp.bfloat16
F32 = jnp.float32


def matmul(left, right):
    return jnp.dot(left, right, preferred_element_type=F32)


def contract_rows(left, right):
    return lax.dot_general(left, right, (((0,), (0,)), ((), ())), preferred_element_type=F32)


def contract_cols(left, right):
    return lax.dot_general(left, right, (((1,), (1,)), ((), ())), preferred_element_type=F32)


def normalize(hidden, gain, shift):
    mean = jnp.mean(hidden, axis=-1, keepdims=True)
    centered = hidden - mean
    inverse = lax.rsqrt(jnp.mean(centered * centered, axis=-1, keepdims=True) + EPS)
    normed = centered * inverse
    return (normed * gain + shift, normed, inverse)


def normalize_back(grad, normed, inverse, gain):
    scaled = grad * gain
    inner = scaled - jnp.mean(scaled, axis=-1, keepdims=True)
    inner = inner - normed * jnp.mean(scaled * normed, axis=-1, keepdims=True)
    return (inverse * inner, jnp.sum(grad * normed, axis=0), jnp.sum(grad, axis=0))


def fill_bias(seg_col, seg_row, bias):
    @pl.when(pl.program_id(0) == 0)
    def _():
        bias[...] = jnp.where(seg_col[...] == seg_row[...], 0.0, NEG)


def head_lanes(head):
    lane = lax.broadcasted_iota(jnp.int32, (TILE, PAIR), 1)
    return lane < HEAD_DIM if head == 0 else lane >= HEAD_DIM


def forward_kernel(seg_col, seg_row, q_ref, k_ref, v_ref, o_ref, lse_ref, bias, out_t):
    fill_bias(seg_col, seg_row, bias)
    keys = k_ref[...]
    values_t = v_ref[...].T
    for tile in range(q_ref.shape[0] // TILE):
        at = slice(tile * TILE, (tile + 1) * TILE)
        query = q_ref[at, :] * jnp.asarray(SCALE, BF)
        for head in range(2):
            mine = jnp.where(head_lanes(head), query, jnp.zeros_like(query))
            scores = contract_cols(keys, mine) + bias[:, at]
            top = jnp.max(scores, axis=0, keepdims=True)
            weights = jnp.exp(scores - top)
            total = jnp.sum(weights, axis=0, keepdims=True)
            probs = (weights * (1.0 / total)).astype(BF)
            rows = slice(head * HEAD_DIM, (head + 1) * HEAD_DIM)
            out_t[rows, at] = matmul(values_t[rows, :], probs)
            lse_ref[0, head : head + 1, at] = top + jnp.log(total)
    o_ref[...] = out_t[...].T.astype(BF)


def backward_kernel(
    seg_col, seg_row, q_ref, k_ref, v_ref, do_ref, lse_ref,
    dq_ref, dk_ref, dv_ref, bq_ref, bv_ref, bias, dq_t, dk_sum, dv_sum,
):
    fill_bias(seg_col, seg_row, bias)
    keys = k_ref[...]
    values = v_ref[...]
    keys_t = keys.T
    for tile in range(q_ref.shape[0] // TILE):
        at = slice(tile * TILE, (tile + 1) * TILE)
        query = q_ref[at, :]
        grad = do_ref[at, :]
        for head in range(2):
            lanes = head_lanes(head)
            query_h = jnp.where(lanes, query, jnp.zeros_like(query))
            grad_h = jnp.where(lanes, grad, jnp.zeros_like(grad))
            scores = contract_cols(keys, query_h * jnp.asarray(SCALE, BF)) + bias[:, at]
            probs = jnp.exp(scores - lse_ref[0, head : head + 1, at])
            grad_probs = contract_cols(values, grad_h)
            inner = jnp.sum(grad_probs * probs, axis=0, keepdims=True)
            grad_scores = (probs * (grad_probs - inner)).astype(BF)
            rows = slice(head * HEAD_DIM, (head + 1) * HEAD_DIM)
            dq_t[rows, at] = matmul(keys_t[rows, :], grad_scores)
            dk_part = matmul(grad_scores, query_h)
            dv_part = matmul(probs.astype(BF), grad_h)
            if tile == 0 and head == 0:
                dk_sum[...] = dk_part
                dv_sum[...] = dv_part
            else:
                dk_sum[...] += dk_part
                dv_sum[...] += dv_part
    dq = (dq_t[...].T * SCALE).astype(BF)
    dv = dv_sum[...].astype(BF)
    dq_ref[...] = dq
    dk_ref[...] = (dk_sum[...] * SCALE).astype(BF)
    dv_ref[...] = dv
    bq_ref[...] = jnp.sum(dq.astype(F32), axis=0, keepdims=True)
    bv_ref[...] = jnp.sum(dv.astype(F32), axis=0, keepdims=True)


def columns(tokens, first):
    return pl.BlockSpec((tokens, PAIR), lambda i: (0, first + i))


def segment_specs(tokens):
    return [pl.BlockSpec((tokens, 1), lambda i: (0, 0)), pl.BlockSpec((1, tokens), lambda i: (0, 0))]


PARAMS = pltpu.CompilerParams(dimension_semantics=("arbitrary",), vmem_limit_bytes=56 * 2**20)


def attend(segments, packed):
    tokens = packed.shape[0]
    width = packed.shape[1] // 3
    pairs = width // PAIR
    return pl.pallas_call(
        forward_kernel,
        grid=(pairs,),
        name="attend",
        in_specs=segment_specs(tokens) + [columns(tokens, part * pairs) for part in range(3)],
        out_specs=[columns(tokens, 0), pl.BlockSpec((1, 2, tokens), lambda i: (i, 0, 0))],
        out_shape=[
            jax.ShapeDtypeStruct((tokens, width), BF),
            jax.ShapeDtypeStruct((pairs, 2, tokens), F32),
        ],
        scratch_shapes=[pltpu.VMEM((tokens, tokens), F32), pltpu.VMEM((PAIR, tokens), F32)],
        compiler_params=PARAMS,
    )(segments.reshape(tokens, 1), segments.reshape(1, tokens), packed, packed, packed)


def attend_back(segments, packed, grad, logsum, chunk):
    tokens = packed.shape[0]
    width = packed.shape[1] // 3
    pairs = width // PAIR
    count = pairs // CHUNKS
    first = chunk * count
    row = pl.BlockSpec((1, PAIR), lambda i: (0, i))
    return pl.pallas_call(
        backward_kernel,
        grid=(count,),
        name="attend_back",
        in_specs=segment_specs(tokens)
        + [columns(tokens, part * pairs + first) for part in range(3)]
        + [columns(tokens, first), pl.BlockSpec((1, 2, tokens), lambda i: (first + i, 0, 0))],
        out_specs=[columns(tokens, 0)] * 3 + [row] * 2,
        out_shape=[jax.ShapeDtypeStruct((tokens, count * PAIR), BF)] * 3
        + [jax.ShapeDtypeStruct((1, count * PAIR), F32)] * 2,
        scratch_shapes=[
            pltpu.VMEM((tokens, tokens), F32),
            pltpu.VMEM((PAIR, tokens), F32),
            pltpu.VMEM((tokens, PAIR), F32),
            pltpu.VMEM((tokens, PAIR), F32),
        ],
        compiler_params=PARAMS,
    )(segments.reshape(tokens, 1), segments.reshape(1, tokens), packed, packed, packed, grad, logsum)


WIDE = 512


def up_kernel(x_ref, w_ref, b_ref, hidden_ref, slope_ref):
    weight = w_ref[...]
    bias = b_ref[...]
    for tile in range(x_ref.shape[0] // TILE):
        at = slice(tile * TILE, (tile + 1) * TILE)
        pre = matmul(x_ref[at, :], weight) + bias
        area = 0.5 * lax.erf(pre * (0.5 ** 0.5)) + 0.5
        hidden_ref[at, :] = (pre * area).astype(BF)
        bell = jnp.exp(pre * pre * -0.5) * BELL
        slope_ref[at, :] = (area + pre * bell).astype(BF)


def up_back_kernel(dz_ref, w_ref, slope_ref, du_ref, sum_ref):
    weight = w_ref[...]
    total = jnp.zeros(sum_ref.shape, F32)
    for tile in range(dz_ref.shape[0] // TILE):
        at = slice(tile * TILE, (tile + 1) * TILE)
        du = (contract_cols(dz_ref[at, :], weight) * slope_ref[at, :].astype(F32)).astype(BF)
        du_ref[at, :] = du
        total += jnp.sum(du.astype(F32), axis=0, keepdims=True)
    sum_ref[...] = total


def up_call(x, packed, bias):
    tokens, width = x.shape
    hidden = bias.shape[0]
    tile = pl.BlockSpec((tokens, WIDE), lambda j: (0, j))
    return pl.pallas_call(up_kernel, grid=(hidden // WIDE,), name="feed",
        in_specs=[pl.BlockSpec((tokens, width), lambda j: (0, 0)),
                  pl.BlockSpec((width, WIDE), lambda j: (0, width // WIDE + j)),
                  pl.BlockSpec((1, WIDE), lambda j: (0, j))],
        out_specs=[tile, tile],
        out_shape=[jax.ShapeDtypeStruct((tokens, hidden), BF)] * 2, compiler_params=PARAMS)(x, packed, bias.reshape(1, hidden))


def up_back_call(dz, weight, slope):
    tokens, width = dz.shape
    hidden = weight.shape[0]
    tile = pl.BlockSpec((tokens, WIDE), lambda j: (0, j))
    return pl.pallas_call(up_back_kernel, grid=(hidden // WIDE,), name="feed_back",
        in_specs=[pl.BlockSpec((tokens, width), lambda j: (0, 0)), pl.BlockSpec((WIDE, width), lambda j: (j, 0)), tile],
        out_specs=[tile, pl.BlockSpec((1, WIDE), lambda j: (0, j))],
        out_shape=[jax.ShapeDtypeStruct((tokens, hidden), BF), jax.ShapeDtypeStruct((1, hidden), F32)], compiler_params=PARAMS)(dz, weight, slope)


def weight_kernel(own_ref, rows_t_ref, q_ref, k_ref, v_ref, keep_ref, send_ref):
    rows_t = rows_t_ref[...]
    share = keep_ref.shape[1]
    step = q_ref.shape[1]
    for part, ref in enumerate((q_ref, k_ref, v_ref)):
        grad = matmul(rows_t, ref[...]).astype(BF).reshape(-1, 2, share, step)
        at = slice(part * step, (part + 1) * step)

        @pl.when(own_ref[0] == 0)
        def _():
            keep_ref[:, :, at] = grad[:, 0]
            send_ref[:, :, at] = grad[:, 1]

        @pl.when(own_ref[0] == 1)
        def _():
            keep_ref[:, :, at] = grad[:, 1]
            send_ref[:, :, at] = grad[:, 0]


def weight_halves(rows_t, parts, devices):
    width, step = rows_t.shape[0], parts[0].shape[1]
    own = (lax.axis_index(AXES) & 1).astype(jnp.int32).reshape(1)
    half = jax.ShapeDtypeStruct((devices // 2, width // devices, 3 * step), BF)
    return pl.pallas_call(
        weight_kernel,
        name="weight_halves",
        in_specs=[pl.BlockSpec(memory_space=pltpu.SMEM)] + [pl.BlockSpec(memory_space=pltpu.VMEM)] * 4,
        out_specs=[pl.BlockSpec(memory_space=pltpu.VMEM)] * 2,
        out_shape=[half, half],
        compiler_params=pltpu.CompilerParams(vmem_limit_bytes=56 * 2**20),
    )(own, rows_t, *parts)


def input_kernel(*refs):
    base_ref, weight_ref, pieces, out_ref = refs[0], refs[1], refs[2:-1], refs[-1]
    width = base_ref.shape[1]
    step = pieces[0].shape[1]
    total = base_ref[...]
    for i, ref in enumerate(pieces):
        first = PAIR + (i % 3) * width + (i // 3) * step
        total += contract_cols(ref[...], weight_ref[:, first : first + step])
    out_ref[...] = total.astype(BF)


def input_call(base, head, pieces):
    tokens, width = base.shape
    step = pieces[0].shape[1]
    row = pl.BlockSpec((TILE, width), lambda i: (i, 0))
    return pl.pallas_call(
        input_kernel,
        grid=(tokens // TILE,),
        name="input_grad",
        in_specs=[row, pl.BlockSpec(head.shape, lambda i: (0, 0))]
        + [pl.BlockSpec((TILE, step), lambda i: (i, 0))] * len(pieces),
        out_specs=row,
        out_shape=jax.ShapeDtypeStruct((tokens, width), BF),
        compiler_params=PARAMS,
    )(base, head, *pieces)


def swap(value, bit, devices):
    return lax.ppermute(value, AXES, [(i, i ^ (1 << bit)) for i in range(devices)])


def bit_orders(bits):
    rest = list(range(1, bits))
    starts = (0, (bits - 1) // 4, (bits - 1) // 2)
    return [[0] + rest[s:] + rest[:s] for s in starts]


def spans(width, parts):
    step = width // PAIR // parts * PAIR
    edges = [step * p for p in range(parts)] + [width]
    return list(zip(edges[:-1], edges[1:]))


class Chain:
    def __init__(self, value, order, devices, kind=BF, pair=None):
        self.devices, self.kind, self.order = devices, kind, list(order)
        self.left = list(range(devices.bit_length() - 1))
        self.bits = len(self.left)
        shape = (2,) * self.bits + (value.shape[0] // devices, value.shape[1])
        self.got = None
        if pair is None:
            self.halve([value.reshape(shape)])
        else:
            self.left.pop()
            self.keep, self.send = (half.reshape(shape[1:]) for half in pair)

    def halve(self, terms):
        bit = self.order[0]
        axis = self.left.index(self.bits - 1 - bit)
        own = (lax.axis_index(AXES) >> bit) & 1
        mine = [lax.dynamic_index_in_dim(t, own, axis, keepdims=False) for t in terms]
        theirs = [lax.dynamic_index_in_dim(t, 1 - own, axis, keepdims=False) for t in terms]
        self.keep = mine[0] if len(terms) == 1 else mine[0].astype(F32) + mine[1].astype(F32)
        send = theirs[0] if len(terms) == 1 else theirs[0].astype(F32) + theirs[1].astype(F32)
        self.send = send.astype(self.kind)
        self.left.pop(axis)

    def begin(self):
        self.got = swap(self.send, self.order.pop(0), self.devices)

    def finish(self):
        got, self.got = self.got, None
        if self.order:
            self.halve([self.keep, got])
        else:
            self.keep, self.send = self.keep.astype(F32) + got.astype(F32), None

    @property
    def over(self):
        return self.send is None


def tick(chains, value):
    active = [c for c in chains if not c.over]
    for c in active:
        if c.got is not None:
            c.finish()
    held = lax.optimization_barrier((value, [(c.keep, c.send) for c in active]))
    for c, (keep, send) in zip(active, held[1]):
        c.keep, c.send = keep, send
        if not c.over:
            c.begin()
    return held[0]


def chains_of(value, devices, parts=3, turn=0, kind=BF):
    orders = bit_orders(devices.bit_length() - 1)
    return [
        Chain(value[:, a:b], orders[(p + turn) % 3], devices, kind)
        for p, (a, b) in enumerate(spans(value.shape[1], parts))
    ]


def result(chains):
    return jnp.concatenate([c.keep for c in chains], axis=1)


def gather_pairs(value, devices, later, parts=3):
    bits = devices.bit_length() - 1
    here = lax.axis_index(AXES)
    orders = [order[::-1] for order in bit_orders(bits)]
    work = [value[:, a:b] for a, b in spans(value.shape[1], parts)]
    held = [[] for _ in range(parts)]
    for step in range(bits):
        for p in range(parts):
            bit = orders[p][step]
            name = bits - 1 - bit
            axis = sum(1 for h in held[p] if h < name)
            own = (here >> bit) & 1
            mine, got = work[p], swap(work[p], bit, devices)
            work[p] = jnp.where(own == 0, jnp.stack([mine, got], axis), jnp.stack([got, mine], axis))
            held[p] = sorted(held[p] + [name])
        if step == bits - 3:
            work, later = lax.optimization_barrier((work, later))
    return [w.reshape(devices * value.shape[0], w.shape[-1]) for w in work], later


def widen(vector):
    return vector.astype(F32)


def local(
    tokens, segment_ids, cotangent, w_query, b_query, w_key, w_value, b_value, w_out, b_out,
    gain_attn, shift_attn, w_up, b_up, w_down, b_down, gain_ffn, shift_ffn, devices,
):
    blocks, length, width = tokens.shape
    rows = tokens.reshape(blocks * length, width)
    rows_t = rows.T
    own = w_query.shape[0]
    ratio = b_up.shape[0] // own
    vectors = [b_query, b_value, b_out, gain_attn, shift_attn, b_down, gain_ffn, shift_ffn]
    names = len(vectors)
    side = jnp.stack(vectors, axis=1)
    side = jnp.concatenate([side, b_up.reshape(own, ratio)], axis=1)
    side = jnp.pad(side, ((0, 0), (0, PAIR - names - ratio)))
    head = jnp.concatenate([side, w_query, w_key, w_value], axis=1).astype(BF)
    later = (jnp.concatenate([w_out, w_up], axis=1).astype(BF), w_down.astype(BF))
    head, later = gather_pairs(head, devices, later)
    head = jnp.concatenate(head, axis=1)
    packed_full = head[:, PAIR:]
    query_bias, value_bias, out_bias, attn_gain, attn_shift, down_bias, ffn_gain, ffn_shift = [
        widen(head[:, i]) for i in range(names)
    ]
    up_bias = widen(head[:, names : names + ratio].reshape(-1))
    out_up = lax.all_gather(later[0], AXES, axis=0, tiled=True)
    down_full = lax.all_gather(later[1], AXES, axis=0, tiled=True)
    out_full, up_full = out_up[:, :width], out_up[:, width:]

    packed_bias = jnp.concatenate([query_bias, jnp.zeros_like(query_bias), value_bias])
    packed = (matmul(rows, packed_full) + packed_bias).astype(BF)
    segments = segment_ids.reshape(-1)
    context, logsums = attend(segments, packed)
    attended = matmul(context, out_full) + out_bias
    first, normed_one, inverse_one = normalize(rows.astype(F32) + attended, attn_gain, attn_shift)
    first_low = first.astype(BF)
    hidden, slope = up_call(first_low, out_up, up_bias)
    branch = matmul(hidden, down_full) + down_bias
    output, normed_two, inverse_two = normalize(first + branch, ffn_gain, ffn_shift)
    encoder_output = output.astype(BF).reshape(tokens.shape)

    incoming = cotangent.reshape(blocks * length, width).astype(F32)
    grad_two, ffn_gain_grad, ffn_shift_grad = normalize_back(incoming, normed_two, inverse_two, ffn_gain)
    grad_branch = grad_two.astype(BF)
    down = chains_of(contract_rows(hidden, grad_branch).astype(BF), devices, parts=2)
    down_bias_grad = jnp.sum(grad_branch.astype(F32), axis=0)
    running = list(down)
    grad_branch = tick(running, grad_branch)
    grad_pre, up_bias_grad = up_back_call(grad_branch, down_full, slope)
    up_bias_grad = up_bias_grad[0]
    grad_pre = tick(running, grad_pre)
    up_product = contract_rows(first_low, grad_pre).astype(BF)
    up = chains_of(up_product, devices, parts=2, turn=2)
    running += up
    grad_pre = tick(running, grad_pre)
    grad_first = grad_two + contract_cols(grad_pre, up_full)
    grad_one, attn_gain_grad, attn_shift_grad = normalize_back(grad_first, normed_one, inverse_one, attn_gain)
    grad_attended = grad_one.astype(BF)
    out_bias_grad = jnp.sum(grad_attended.astype(F32), axis=0)
    grad_attended = tick(running, grad_attended)
    out_product = contract_rows(context, grad_attended).astype(BF)
    out = chains_of(out_product, devices, parts=1, turn=2)
    grad_context = contract_cols(grad_attended, out_full).astype(BF)
    running += out

    pieces, shares = [], []
    for chunk in range(CHUNKS):
        grad_context = tick(running, grad_context)
        piece = attend_back(segments, packed, grad_context, logsums, chunk)
        if chunk + 1 < CHUNKS:
            grad_context, piece = lax.optimization_barrier((grad_context, piece))
        pieces.append(piece)
        if own % 32 == 0:
            pair = weight_halves(rows_t, piece[:3], devices)
            order = bit_orders(devices.bit_length() - 1)[chunk % 3]
            grads = jax.ShapeDtypeStruct((width, pair[0].shape[2]), BF)
            shares.append([Chain(grads, order, devices, pair=pair)])
        else:
            grads = jnp.concatenate([matmul(rows_t, part).astype(BF) for part in piece[:3]], axis=1)
            shares.append(chains_of(grads, devices, parts=1, turn=chunk))
        running += shares[-1]
    joined = {part: jnp.concatenate([piece[part] for piece in pieces], axis=1) for part in (3, 4)}
    vector_grads = [
        joined[3][0], joined[4][0], out_bias_grad, attn_gain_grad, attn_shift_grad,
        down_bias_grad, ffn_gain_grad, ffn_shift_grad,
    ]
    side_grad = jnp.concatenate(
        [v.reshape(devices, own) for v in vector_grads] + [up_bias_grad.reshape(devices, own * ratio)],
        axis=1,
    )
    side = chains_of(side_grad, devices, parts=1, kind=F32)
    running += side
    pieces = tick(running, [part for piece in pieces for part in piece[:3]])
    total_input = input_call(grad_one, head, pieces)
    layer_input_gradient = total_input.reshape(tokens.shape)
    while not all(c.over for c in running):
        tick(running, ())

    down_grad, up_grad, out_grad = result(down), result(up), result(out)
    shares = [result(share) for share in shares]
    step = width // CHUNKS
    query_grad, key_grad, value_grad = [
        jnp.concatenate([share[:, part * step : (part + 1) * step] for share in shares], axis=1)
        for part in range(3)
    ]
    side_grad = result(side)[0]
    parts = [side_grad[i * own : (i + 1) * own] for i in range(names)]
    up_bias_share = side_grad[names * own :]
    return (
        encoder_output, layer_input_gradient, query_grad, parts[0], key_grad, value_grad, parts[1],
        out_grad, parts[2], parts[3], parts[4], up_grad, up_bias_share, down_grad, parts[5],
        parts[6], parts[7],
    )


def solution(mesh):
    devices = mesh.shape["fsdp"] * mesh.shape["rep"]
    act, ids = P("rep", "fsdp", None), P("rep", "fsdp")
    mat, vec = P(AXES, None), P(AXES)
    return jax.shard_map(
        partial(local, devices=devices),
        mesh=mesh,
        in_specs=(
            act, ids, act, mat, vec, mat, mat, vec, mat, vec, vec, vec, mat, vec, mat, vec, vec, vec,
        ),
        out_specs=(act, act, mat, vec, mat, mat, vec, mat, vec, vec, vec, mat, vec, mat, vec, vec, vec),
        check_vma=False,
    )
```

```python
from functools import partial

import jax
import jax.numpy as jnp
from jax import lax
from jax.experimental import pallas as pl
from jax.experimental.pallas import tpu as pltpu
from jax.sharding import PartitionSpec as P


HEAD_DIM = 64
PAIR = 128
TILE = 256
CHUNKS = 4
SCALE = 0.125
EPS = 1e-05
NEG = -1e30
BELL = (2.0 * 3.141592653589793) ** -0.5
AXES = ("fsdp", "rep")
BF = jnp.bfloat16
F32 = jnp.float32


def matmul(left, right):
    return jnp.dot(left, right, preferred_element_type=F32)


def contract_rows(left, right):
    return lax.dot_general(left, right, (((0,), (0,)), ((), ())), preferred_element_type=F32)


def contract_cols(left, right):
    return lax.dot_general(left, right, (((1,), (1,)), ((), ())), preferred_element_type=F32)


def normalize(hidden, gain, shift):
    mean = jnp.mean(hidden, axis=-1, keepdims=True)
    centered = hidden - mean
    inverse = lax.rsqrt(jnp.mean(centered * centered, axis=-1, keepdims=True) + EPS)
    normed = centered * inverse
    return (normed * gain + shift, normed, inverse)


def normalize_back(grad, normed, inverse, gain):
    scaled = grad * gain
    inner = scaled - jnp.mean(scaled, axis=-1, keepdims=True)
    inner = inner - normed * jnp.mean(scaled * normed, axis=-1, keepdims=True)
    return (inverse * inner, jnp.sum(grad * normed, axis=0), jnp.sum(grad, axis=0))


def fill_bias(seg_col, seg_row, bias):
    @pl.when(pl.program_id(0) == 0)
    def _():
        bias[...] = jnp.where(seg_col[...] == seg_row[...], 0.0, NEG)


def head_lanes(head):
    lane = lax.broadcasted_iota(jnp.int32, (TILE, PAIR), 1)
    return lane < HEAD_DIM if head == 0 else lane >= HEAD_DIM


def forward_kernel(seg_col, seg_row, q_ref, k_ref, v_ref, o_ref, lse_ref, bias, out_t):
    fill_bias(seg_col, seg_row, bias)
    keys = k_ref[...]
    values_t = v_ref[...].T
    for tile in range(q_ref.shape[0] // TILE):
        at = slice(tile * TILE, (tile + 1) * TILE)
        query = q_ref[at, :] * jnp.asarray(SCALE, BF)
        for head in range(2):
            mine = jnp.where(head_lanes(head), query, jnp.zeros_like(query))
            scores = contract_cols(keys, mine) + bias[:, at]
            top = jnp.max(scores, axis=0, keepdims=True)
            weights = jnp.exp(scores - top)
            total = jnp.sum(weights, axis=0, keepdims=True)
            rows = slice(head * HEAD_DIM, (head + 1) * HEAD_DIM)
            out_t[rows, at] = matmul(values_t[rows, :], weights.astype(BF)) * (1.0 / total)
            lse_ref[0, head : head + 1, at] = top + jnp.log(total)
    o_ref[...] = out_t[...].T.astype(BF)


def backward_kernel(
    seg_col, seg_row, q_ref, k_ref, v_ref, do_ref, lse_ref,
    grads_ref, bq_ref, bv_ref, bias, dq_t, dk_sum, dv_sum,
):
    fill_bias(seg_col, seg_row, bias)
    keys = k_ref[...]
    values = v_ref[...]
    keys_t = keys.T
    for tile in range(q_ref.shape[0] // TILE):
        at = slice(tile * TILE, (tile + 1) * TILE)
        query = q_ref[at, :]
        grad = do_ref[at, :]
        for head in range(2):
            lanes = head_lanes(head)
            query_h = jnp.where(lanes, query, jnp.zeros_like(query))
            grad_h = jnp.where(lanes, grad, jnp.zeros_like(grad))
            scores = contract_cols(keys, query_h * jnp.asarray(SCALE, BF)) + bias[:, at]
            probs = jnp.exp(scores - lse_ref[0, head : head + 1, at])
            grad_probs = contract_cols(values, grad_h)
            inner = jnp.sum(grad_probs * probs, axis=0, keepdims=True)
            grad_scores = (probs * (grad_probs - inner)).astype(BF)
            rows = slice(head * HEAD_DIM, (head + 1) * HEAD_DIM)
            dq_t[rows, at] = matmul(keys_t[rows, :], grad_scores)
            dk_part = matmul(grad_scores, query_h)
            dv_part = matmul(probs.astype(BF), grad_h)
            if tile == 0 and head == 0:
                dk_sum[...] = dk_part
                dv_sum[...] = dv_part
            else:
                dk_sum[...] += dk_part
                dv_sum[...] += dv_part
    dq = (dq_t[...].T * SCALE).astype(BF)
    dv = dv_sum[...].astype(BF)
    grads_ref[0] = dq
    grads_ref[1] = (dk_sum[...] * SCALE).astype(BF)
    grads_ref[2] = dv
    bq_ref[...] = jnp.sum(dq.astype(F32), axis=0, keepdims=True)
    bv_ref[...] = jnp.sum(dv.astype(F32), axis=0, keepdims=True)


def columns(tokens, first):
    return pl.BlockSpec((tokens, PAIR), lambda i: (0, first + i))


def segment_specs(tokens):
    return [pl.BlockSpec((tokens, 1), lambda i: (0, 0)), pl.BlockSpec((1, tokens), lambda i: (0, 0))]


PARAMS = pltpu.CompilerParams(dimension_semantics=("arbitrary",), vmem_limit_bytes=56 * 2**20)


def attend(segments, packed):
    tokens = packed.shape[0]
    width = packed.shape[1] // 3
    pairs = width // PAIR
    return pl.pallas_call(
        forward_kernel,
        grid=(pairs,),
        name="attend",
        in_specs=segment_specs(tokens) + [columns(tokens, part * pairs) for part in range(3)],
        out_specs=[columns(tokens, 0), pl.BlockSpec((1, 2, tokens), lambda i: (i, 0, 0))],
        out_shape=[
            jax.ShapeDtypeStruct((tokens, width), BF),
            jax.ShapeDtypeStruct((pairs, 2, tokens), F32),
        ],
        scratch_shapes=[pltpu.VMEM((tokens, tokens), F32), pltpu.VMEM((PAIR, tokens), F32)],
        compiler_params=PARAMS,
    )(segments.reshape(tokens, 1), segments.reshape(1, tokens), packed, packed, packed)


def attend_back(segments, packed, grad, logsum, chunk):
    tokens = packed.shape[0]
    width = packed.shape[1] // 3
    pairs = width // PAIR
    count = pairs // CHUNKS
    first = chunk * count
    row = pl.BlockSpec((1, PAIR), lambda i: (0, i))
    return pl.pallas_call(
        backward_kernel,
        grid=(count,),
        name="attend_back",
        in_specs=segment_specs(tokens)
        + [columns(tokens, part * pairs + first) for part in range(3)]
        + [columns(tokens, first), pl.BlockSpec((1, 2, tokens), lambda i: (first + i, 0, 0))],
        out_specs=[pl.BlockSpec((3, tokens, PAIR), lambda i: (0, 0, i))] + [row] * 2,
        out_shape=[jax.ShapeDtypeStruct((3, tokens, count * PAIR), BF)]
        + [jax.ShapeDtypeStruct((1, count * PAIR), F32)] * 2,
        scratch_shapes=[
            pltpu.VMEM((tokens, tokens), F32),
            pltpu.VMEM((PAIR, tokens), F32),
            pltpu.VMEM((tokens, PAIR), F32),
            pltpu.VMEM((tokens, PAIR), F32),
        ],
        compiler_params=PARAMS,
    )(segments.reshape(tokens, 1), segments.reshape(1, tokens), packed, packed, packed, grad, logsum)


WIDE = 512


def up_kernel(x_ref, w_ref, b_ref, hidden_ref, slope_ref):
    weight = w_ref[...]
    bias = b_ref[...]
    for tile in range(x_ref.shape[0] // TILE):
        at = slice(tile * TILE, (tile + 1) * TILE)
        pre = matmul(x_ref[at, :], weight) + bias
        area = 0.5 * lax.erf(pre * (0.5 ** 0.5)) + 0.5
        hidden_ref[at, :] = (pre * area).astype(BF)
        bell = jnp.exp(pre * pre * -0.5) * BELL
        slope_ref[at, :] = (area + pre * bell).astype(BF)


def up_back_kernel(dz_ref, w_ref, slope_ref, du_ref, sum_ref):
    weight = w_ref[...]
    total = jnp.zeros(sum_ref.shape, F32)
    for tile in range(dz_ref.shape[0] // TILE):
        at = slice(tile * TILE, (tile + 1) * TILE)
        du = (contract_cols(dz_ref[at, :], weight) * slope_ref[at, :].astype(F32)).astype(BF)
        du_ref[at, :] = du
        total += jnp.sum(du.astype(F32), axis=0, keepdims=True)
    sum_ref[...] = total


def up_call(x, packed, bias):
    tokens, width = x.shape
    hidden = bias.shape[0]
    tile = pl.BlockSpec((tokens, WIDE), lambda j: (0, j))
    return pl.pallas_call(up_kernel, grid=(hidden // WIDE,), name="feed",
        in_specs=[pl.BlockSpec((tokens, width), lambda j: (0, 0)),
                  pl.BlockSpec((width, WIDE), lambda j: (0, width // WIDE + j)),
                  pl.BlockSpec((1, WIDE), lambda j: (0, j))],
        out_specs=[tile, tile],
        out_shape=[jax.ShapeDtypeStruct((tokens, hidden), BF)] * 2, compiler_params=PARAMS)(x, packed, bias.reshape(1, hidden))


def up_back_call(dz, weight, slope):
    tokens, width = dz.shape
    hidden = weight.shape[0]
    tile = pl.BlockSpec((tokens, WIDE), lambda j: (0, j))
    return pl.pallas_call(up_back_kernel, grid=(hidden // WIDE,), name="feed_back",
        in_specs=[pl.BlockSpec((tokens, width), lambda j: (0, 0)), pl.BlockSpec((WIDE, width), lambda j: (j, 0)), tile],
        out_specs=[tile, pl.BlockSpec((1, WIDE), lambda j: (0, j))],
        out_shape=[jax.ShapeDtypeStruct((tokens, hidden), BF), jax.ShapeDtypeStruct((1, hidden), F32)], compiler_params=PARAMS)(dz, weight, slope)


def weight_kernel(own_ref, rows_t_ref, part_ref, keep_ref, send_ref):
    share, step = keep_ref.shape[1:]
    grad = matmul(rows_t_ref[...], part_ref[0]).astype(BF).reshape(-1, 2, share, step)

    @pl.when(own_ref[0] == 0)
    def _():
        keep_ref[...] = grad[:, 0]
        send_ref[...] = grad[:, 1]

    @pl.when(own_ref[0] == 1)
    def _():
        keep_ref[...] = grad[:, 1]
        send_ref[...] = grad[:, 0]


def weight_halves(rows_t, parts, devices):
    (width, tokens), step = rows_t.shape, parts.shape[2]
    own = (lax.axis_index(AXES) & 1).astype(jnp.int32).reshape(1)
    half = (devices // 2, width // devices)
    spec = pl.BlockSpec(half + (step,), lambda i: (0, 0, i))
    return pl.pallas_call(
        weight_kernel,
        grid=(3,),
        name="weight_halves",
        in_specs=[
            pl.BlockSpec(memory_space=pltpu.SMEM),
            pl.BlockSpec((width, tokens), lambda i: (0, 0)),
            pl.BlockSpec((1, tokens, step), lambda i: (i, 0, 0)),
        ],
        out_specs=[spec, spec],
        out_shape=[jax.ShapeDtypeStruct(half + (3 * step,), BF)] * 2,
        compiler_params=PARAMS,
    )(own, rows_t, parts)


def input_kernel(*refs):
    base_ref, weight_ref, pieces, out_ref = refs[0], refs[1], refs[2:-1], refs[-1]
    width = base_ref.shape[1]
    step = pieces[0].shape[2]
    total = base_ref[...]
    for i, ref in enumerate(pieces):
        for part in range(3):
            first = PAIR + part * width + i * step
            total += contract_cols(ref[part], weight_ref[:, first : first + step])
    out_ref[...] = total.astype(BF)


def input_call(base, head, pieces):
    tokens, width = base.shape
    step = pieces[0].shape[2]
    row = pl.BlockSpec((TILE, width), lambda i: (i, 0))
    return pl.pallas_call(
        input_kernel,
        grid=(tokens // TILE,),
        name="input_grad",
        in_specs=[row, pl.BlockSpec(head.shape, lambda i: (0, 0))]
        + [pl.BlockSpec((3, TILE, step), lambda i: (0, i, 0))] * len(pieces),
        out_specs=row,
        out_shape=jax.ShapeDtypeStruct((tokens, width), BF),
        compiler_params=PARAMS,
    )(base, head, *pieces)


def swap(value, bit, devices):
    return lax.ppermute(value, AXES, [(i, i ^ (1 << bit)) for i in range(devices)])


def bit_orders(bits):
    rest = list(range(1, bits))
    starts = (0, (bits - 1) // 4, (bits - 1) // 2)
    return [[0] + rest[s:] + rest[:s] for s in starts]


def spans(width, parts):
    step = width // PAIR // parts * PAIR
    edges = [step * p for p in range(parts)] + [width]
    return list(zip(edges[:-1], edges[1:]))


class Chain:
    def __init__(self, value, order, devices, kind=BF, pair=None):
        self.devices, self.kind, self.order = devices, kind, list(order)
        self.left = list(range(devices.bit_length() - 1))
        self.bits = len(self.left)
        shape = (2,) * self.bits + (value.shape[0] // devices, value.shape[1])
        self.got = None
        if pair is None:
            self.halve([value.reshape(shape)])
        else:
            self.left.pop()
            self.keep, self.send = (half.reshape(shape[1:]) for half in pair)

    def halve(self, terms):
        bit = self.order[0]
        axis = self.left.index(self.bits - 1 - bit)
        own = (lax.axis_index(AXES) >> bit) & 1
        mine = [lax.dynamic_index_in_dim(t, own, axis, keepdims=False) for t in terms]
        theirs = [lax.dynamic_index_in_dim(t, 1 - own, axis, keepdims=False) for t in terms]
        self.keep = mine[0] if len(terms) == 1 else mine[0].astype(F32) + mine[1].astype(F32)
        send = theirs[0] if len(terms) == 1 else theirs[0].astype(F32) + theirs[1].astype(F32)
        self.send = send.astype(self.kind)
        self.left.pop(axis)

    def begin(self):
        self.got = swap(self.send, self.order.pop(0), self.devices)

    def finish(self):
        got, self.got = self.got, None
        if self.order:
            self.halve([self.keep, got])
        else:
            self.keep, self.send = self.keep.astype(F32) + got.astype(F32), None

    @property
    def over(self):
        return self.send is None


def tick(chains, value):
    active = [c for c in chains if not c.over]
    for c in active:
        if c.got is not None:
            c.finish()
    held = lax.optimization_barrier((value, [(c.keep, c.send) for c in active]))
    for c, (keep, send) in zip(active, held[1]):
        c.keep, c.send = keep, send
        if not c.over:
            c.begin()
    return held[0]


def chains_of(value, devices, parts=3, turn=0, kind=BF):
    orders = bit_orders(devices.bit_length() - 1)
    return [
        Chain(value[:, a:b], orders[(p + turn) % 3], devices, kind)
        for p, (a, b) in enumerate(spans(value.shape[1], parts))
    ]


def result(chains):
    return jnp.concatenate([c.keep for c in chains], axis=1)


def gather_pairs(value, devices, later, parts=3):
    bits = devices.bit_length() - 1
    here = lax.axis_index(AXES)
    orders = [order[::-1] for order in bit_orders(bits)]
    work = [value[:, a:b] for a, b in spans(value.shape[1], parts)]
    held = [[] for _ in range(parts)]
    for step in range(bits):
        for p in range(parts):
            bit = orders[p][step]
            name = bits - 1 - bit
            axis = sum(1 for h in held[p] if h < name)
            own = (here >> bit) & 1
            mine, got = work[p], swap(work[p], bit, devices)
            work[p] = jnp.where(own == 0, jnp.stack([mine, got], axis), jnp.stack([got, mine], axis))
            held[p] = sorted(held[p] + [name])
        if step == bits - 3:
            work, later = lax.optimization_barrier((work, later))
    return [w.reshape(devices * value.shape[0], w.shape[-1]) for w in work], later


def widen(vector):
    return vector.astype(F32)


def local(
    tokens, segment_ids, cotangent, w_query, b_query, w_key, w_value, b_value, w_out, b_out,
    gain_attn, shift_attn, w_up, b_up, w_down, b_down, gain_ffn, shift_ffn, devices,
):
    blocks, length, width = tokens.shape
    rows = tokens.reshape(blocks * length, width)
    rows_t = rows.T
    own = w_query.shape[0]
    ratio = b_up.shape[0] // own
    vectors = [b_query, b_value, b_out, gain_attn, shift_attn, b_down, gain_ffn, shift_ffn]
    names = len(vectors)
    side = jnp.stack(vectors, axis=1)
    side = jnp.concatenate([side, b_up.reshape(own, ratio)], axis=1)
    side = jnp.pad(side, ((0, 0), (0, PAIR - names - ratio)))
    head = jnp.concatenate([side, w_query, w_key, w_value], axis=1).astype(BF)
    later = (jnp.concatenate([w_out, w_up], axis=1).astype(BF), w_down.astype(BF))
    head, later = gather_pairs(head, devices, later)
    head = jnp.concatenate(head, axis=1)
    packed_full = head[:, PAIR:]
    query_bias, value_bias, out_bias, attn_gain, attn_shift, down_bias, ffn_gain, ffn_shift = [
        widen(head[:, i]) for i in range(names)
    ]
    up_bias = widen(head[:, names : names + ratio].reshape(-1))
    out_up = lax.all_gather(later[0], AXES, axis=0, tiled=True)
    down_full = lax.all_gather(later[1], AXES, axis=0, tiled=True)
    out_full, up_full = out_up[:, :width], out_up[:, width:]

    packed_bias = jnp.concatenate([query_bias, jnp.zeros_like(query_bias), value_bias])
    packed = (matmul(rows, packed_full) + packed_bias).astype(BF)
    segments = segment_ids.reshape(-1)
    context, logsums = attend(segments, packed)
    attended = matmul(context, out_full) + out_bias
    first, normed_one, inverse_one = normalize(rows.astype(F32) + attended, attn_gain, attn_shift)
    first_low = first.astype(BF)
    hidden, slope = up_call(first_low, out_up, up_bias)
    branch = matmul(hidden, down_full) + down_bias
    output, normed_two, inverse_two = normalize(first + branch, ffn_gain, ffn_shift)
    encoder_output = output.astype(BF).reshape(tokens.shape)

    incoming = cotangent.reshape(blocks * length, width).astype(F32)
    grad_two, ffn_gain_grad, ffn_shift_grad = normalize_back(incoming, normed_two, inverse_two, ffn_gain)
    grad_branch = grad_two.astype(BF)
    down = chains_of(contract_rows(hidden, grad_branch).astype(BF), devices, parts=2)
    down_bias_grad = jnp.sum(grad_branch.astype(F32), axis=0)
    running = list(down)
    grad_branch = tick(running, grad_branch)
    grad_pre, up_bias_grad = up_back_call(grad_branch, down_full, slope)
    up_bias_grad = up_bias_grad[0]
    grad_pre = tick(running, grad_pre)
    up_product = contract_rows(first_low, grad_pre).astype(BF)
    up = chains_of(up_product, devices, parts=2, turn=2)
    running += up
    grad_pre = tick(running, grad_pre)
    grad_first = grad_two + contract_cols(grad_pre, up_full)
    grad_one, attn_gain_grad, attn_shift_grad = normalize_back(
        grad_first, normed_one, inverse_one, attn_gain
    )
    grad_attended = grad_one.astype(BF)
    out_bias_grad = jnp.sum(grad_attended.astype(F32), axis=0)
    out_product = contract_rows(context, grad_attended).astype(BF)
    out = chains_of(out_product, devices, parts=1, turn=2)
    grad_context = contract_cols(grad_attended, out_full).astype(BF)
    running += out

    pieces, shares = [], []
    for chunk in range(CHUNKS):
        grad_context = tick(running, grad_context)
        piece = attend_back(segments, packed, grad_context, logsums, chunk)
        if chunk + 1 < CHUNKS:
            grad_context, piece = lax.optimization_barrier((grad_context, piece))
        pieces.append(piece)
        if own % 32 == 0:
            pair = weight_halves(rows_t, piece[0], devices)
            order = bit_orders(devices.bit_length() - 1)[chunk % 3]
            grads = jax.ShapeDtypeStruct((width, pair[0].shape[2]), BF)
            shares.append([Chain(grads, order, devices, pair=pair)])
        else:
            grads = jnp.concatenate([matmul(rows_t, piece[0][part]).astype(BF) for part in range(3)], axis=1)
            shares.append(chains_of(grads, devices, parts=1, turn=chunk))
        running += shares[-1]
    joined = [jnp.concatenate([piece[part] for piece in pieces], axis=1) for part in (1, 2)]
    vector_grads = [
        joined[0][0], joined[1][0], out_bias_grad, attn_gain_grad, attn_shift_grad,
        down_bias_grad, ffn_gain_grad, ffn_shift_grad,
    ]
    side_grad = jnp.concatenate(
        [v.reshape(devices, own) for v in vector_grads] + [up_bias_grad.reshape(devices, own * ratio)],
        axis=1,
    )
    side = chains_of(side_grad, devices, parts=1, kind=F32)
    running += side
    tick(running, ())
    pieces = tick(running, [piece[0] for piece in pieces])
    total_input = input_call(grad_one, head, pieces)
    layer_input_gradient = total_input.reshape(tokens.shape)
    while not all(c.over for c in running):
        tick(running, ())

    down_grad, up_grad, out_grad = result(down), result(up), result(out)
    shares = [result(share) for share in shares]
    step = width // CHUNKS
    query_grad, key_grad, value_grad = [
        jnp.concatenate([share[:, part * step : (part + 1) * step] for share in shares], axis=1)
        for part in range(3)
    ]
    side_grad = result(side)[0]
    parts = [side_grad[i * own : (i + 1) * own] for i in range(names)]
    up_bias_share = side_grad[names * own :]
    return (
        encoder_output, layer_input_gradient, query_grad, parts[0], key_grad, value_grad, parts[1],
        out_grad, parts[2], parts[3], parts[4], up_grad, up_bias_share, down_grad, parts[5],
        parts[6], parts[7],
    )


def solution(mesh):
    devices = mesh.shape["fsdp"] * mesh.shape["rep"]
    act, ids = P("rep", "fsdp", None), P("rep", "fsdp")
    mat, vec = P(AXES, None), P(AXES)
    return jax.shard_map(
        partial(local, devices=devices),
        mesh=mesh,
        in_specs=(
            act, ids, act, mat, vec, mat, mat, vec, mat, vec, vec, vec, mat, vec, mat, vec, vec, vec,
        ),
        out_specs=(act, act, mat, vec, mat, mat, vec, mat, vec, vec, vec, mat, vec, mat, vec, vec, vec),
        check_vma=False,
    )
```

```python
from functools import partial

import jax
import jax.numpy as jnp
from jax import lax
from jax.experimental import pallas as pl
from jax.experimental.pallas import tpu as pltpu
from jax.sharding import PartitionSpec as P


HEAD_DIM = 64
PAIR = 128
TILE = 256
CHUNKS = 4
SCALE = 0.125
EPS = 1e-05
NEG = -1e30
BELL = (2.0 * 3.141592653589793) ** -0.5
AXES = ("fsdp", "rep")
BF = jnp.bfloat16
F32 = jnp.float32


def matmul(left, right):
    return jnp.dot(left, right, preferred_element_type=F32)


def contract_rows(left, right):
    return lax.dot_general(left, right, (((0,), (0,)), ((), ())), preferred_element_type=F32)


def contract_cols(left, right):
    return lax.dot_general(left, right, (((1,), (1,)), ((), ())), preferred_element_type=F32)


def normalize(hidden, gain, shift):
    mean = jnp.mean(hidden, axis=-1, keepdims=True)
    centered = hidden - mean
    inverse = lax.rsqrt(jnp.mean(centered * centered, axis=-1, keepdims=True) + EPS)
    normed = centered * inverse
    return (normed * gain + shift, normed, inverse)


def normalize_back(grad, normed, inverse, gain):
    scaled = grad * gain
    inner = scaled - jnp.mean(scaled, axis=-1, keepdims=True)
    inner = inner - normed * jnp.mean(scaled * normed, axis=-1, keepdims=True)
    return (inverse * inner, jnp.sum(grad * normed, axis=0), jnp.sum(grad, axis=0))


def fill_bias(seg_col, seg_row, bias):
    @pl.when(pl.program_id(0) == 0)
    def _():
        bias[...] = jnp.where(seg_col[...] == seg_row[...], 0.0, NEG)


def head_lanes(head):
    lane = lax.broadcasted_iota(jnp.int32, (TILE, PAIR), 1)
    return lane < HEAD_DIM if head == 0 else lane >= HEAD_DIM


def forward_kernel(seg_col, seg_row, q_ref, k_ref, v_ref, o_ref, lse_ref, bias, out_t):
    fill_bias(seg_col, seg_row, bias)
    keys = k_ref[...]
    values_t = v_ref[...].T
    for tile in range(q_ref.shape[0] // TILE):
        at = slice(tile * TILE, (tile + 1) * TILE)
        query = q_ref[at, :] * jnp.asarray(SCALE, BF)
        for head in range(2):
            mine = jnp.where(head_lanes(head), query, jnp.zeros_like(query))
            scores = contract_cols(keys, mine) + bias[:, at]
            top = jnp.max(scores, axis=0, keepdims=True)
            weights = jnp.exp(scores - top)
            total = jnp.sum(weights, axis=0, keepdims=True)
            rows = slice(head * HEAD_DIM, (head + 1) * HEAD_DIM)
            out_t[rows, at] = matmul(values_t[rows, :], weights.astype(BF)) * (1.0 / total)
            lse_ref[0, head : head + 1, at] = top + jnp.log(total)
    o_ref[...] = out_t[...].T.astype(BF)


def backward_kernel(
    seg_col, seg_row, q_ref, k_ref, v_ref, do_ref, lse_ref,
    grads_ref, bq_ref, bv_ref, bias, dq_t, dk_sum, dv_sum,
):
    fill_bias(seg_col, seg_row, bias)
    keys = k_ref[...]
    values = v_ref[...]
    keys_t = keys.T
    for tile in range(q_ref.shape[0] // TILE):
        at = slice(tile * TILE, (tile + 1) * TILE)
        query = q_ref[at, :]
        grad = do_ref[at, :]
        for head in range(2):
            lanes = head_lanes(head)
            query_h = jnp.where(lanes, query, jnp.zeros_like(query))
            grad_h = jnp.where(lanes, grad, jnp.zeros_like(grad))
            scores = contract_cols(keys, query_h * jnp.asarray(SCALE, BF)) + bias[:, at]
            probs = jnp.exp(scores - lse_ref[0, head : head + 1, at])
            grad_probs = contract_cols(values, grad_h)
            inner = jnp.sum(grad_probs * probs, axis=0, keepdims=True)
            grad_scores = (probs * (grad_probs - inner)).astype(BF)
            rows = slice(head * HEAD_DIM, (head + 1) * HEAD_DIM)
            dq_t[rows, at] = matmul(keys_t[rows, :], grad_scores)
            dk_part = matmul(grad_scores, query_h)
            dv_part = matmul(probs.astype(BF), grad_h)
            if tile == 0 and head == 0:
                dk_sum[...] = dk_part
                dv_sum[...] = dv_part
            else:
                dk_sum[...] += dk_part
                dv_sum[...] += dv_part
    dq = (dq_t[...].T * SCALE).astype(BF)
    dv = dv_sum[...].astype(BF)
    grads_ref[0] = dq
    grads_ref[1] = (dk_sum[...] * SCALE).astype(BF)
    grads_ref[2] = dv
    bq_ref[...] = jnp.sum(dq.astype(F32), axis=0, keepdims=True)
    bv_ref[...] = jnp.sum(dv.astype(F32), axis=0, keepdims=True)


def columns(tokens, first):
    return pl.BlockSpec((tokens, PAIR), lambda i: (0, first + i))


def segment_specs(tokens):
    return [pl.BlockSpec((tokens, 1), lambda i: (0, 0)), pl.BlockSpec((1, tokens), lambda i: (0, 0))]


PARAMS = pltpu.CompilerParams(dimension_semantics=("arbitrary",), vmem_limit_bytes=56 * 2**20)


def attend(segments, packed):
    tokens = packed.shape[0]
    width = packed.shape[1] // 3
    pairs = width // PAIR
    return pl.pallas_call(
        forward_kernel,
        grid=(pairs,),
        name="attend",
        in_specs=segment_specs(tokens) + [columns(tokens, part * pairs) for part in range(3)],
        out_specs=[columns(tokens, 0), pl.BlockSpec((1, 2, tokens), lambda i: (i, 0, 0))],
        out_shape=[
            jax.ShapeDtypeStruct((tokens, width), BF),
            jax.ShapeDtypeStruct((pairs, 2, tokens), F32),
        ],
        scratch_shapes=[pltpu.VMEM((tokens, tokens), F32), pltpu.VMEM((PAIR, tokens), F32)],
        compiler_params=PARAMS,
    )(segments.reshape(tokens, 1), segments.reshape(1, tokens), packed, packed, packed)


def attend_back(segments, packed, grad, logsum, chunk):
    tokens = packed.shape[0]
    width = packed.shape[1] // 3
    pairs = width // PAIR
    count = pairs // CHUNKS
    first = chunk * count
    row = pl.BlockSpec((1, PAIR), lambda i: (0, i))
    return pl.pallas_call(
        backward_kernel,
        grid=(count,),
        name="attend_back",
        in_specs=segment_specs(tokens)
        + [columns(tokens, part * pairs + first) for part in range(3)]
        + [columns(tokens, first), pl.BlockSpec((1, 2, tokens), lambda i: (first + i, 0, 0))],
        out_specs=[pl.BlockSpec((3, tokens, PAIR), lambda i: (0, 0, i))] + [row] * 2,
        out_shape=[jax.ShapeDtypeStruct((3, tokens, count * PAIR), BF)]
        + [jax.ShapeDtypeStruct((1, count * PAIR), F32)] * 2,
        scratch_shapes=[
            pltpu.VMEM((tokens, tokens), F32),
            pltpu.VMEM((PAIR, tokens), F32),
            pltpu.VMEM((tokens, PAIR), F32),
            pltpu.VMEM((tokens, PAIR), F32),
        ],
        compiler_params=PARAMS,
    )(segments.reshape(tokens, 1), segments.reshape(1, tokens), packed, packed, packed, grad, logsum)


WIDE = 512


def up_kernel(x_ref, w_ref, b_ref, hidden_ref, slope_ref):
    weight = w_ref[...]
    bias = b_ref[...]
    for tile in range(x_ref.shape[0] // TILE):
        at = slice(tile * TILE, (tile + 1) * TILE)
        pre = matmul(x_ref[at, :], weight) + bias
        area = 0.5 * lax.erf(pre * (0.5 ** 0.5)) + 0.5
        hidden_ref[at, :] = (pre * area).astype(BF)
        bell = jnp.exp(pre * pre * -0.5) * BELL
        slope_ref[at, :] = (area + pre * bell).astype(BF)


def up_back_kernel(dz_ref, w_ref, slope_ref, du_ref, sum_ref):
    weight = w_ref[...]
    total = jnp.zeros(sum_ref.shape, F32)
    for tile in range(dz_ref.shape[0] // TILE):
        at = slice(tile * TILE, (tile + 1) * TILE)
        du = (contract_cols(dz_ref[at, :], weight) * slope_ref[at, :].astype(F32)).astype(BF)
        du_ref[at, :] = du
        total += jnp.sum(du.astype(F32), axis=0, keepdims=True)
    sum_ref[...] = total


def up_call(x, packed, bias):
    tokens, width = x.shape
    hidden = bias.shape[0]
    tile = pl.BlockSpec((tokens, WIDE), lambda j: (0, j))
    return pl.pallas_call(up_kernel, grid=(hidden // WIDE,), name="feed",
        in_specs=[pl.BlockSpec((tokens, width), lambda j: (0, 0)),
                  pl.BlockSpec((width, WIDE), lambda j: (0, hidden // WIDE + j)),
                  pl.BlockSpec((1, WIDE), lambda j: (0, j))],
        out_specs=[tile, tile],
        out_shape=[jax.ShapeDtypeStruct((tokens, hidden), BF)] * 2, compiler_params=PARAMS)(x, packed, bias.reshape(1, hidden))


def up_back_call(dz, weight, slope):
    tokens, width = dz.shape
    hidden = slope.shape[1]
    halves = width // WIDE
    tile = pl.BlockSpec((tokens, WIDE), lambda j: (0, j))
    return pl.pallas_call(up_back_kernel, grid=(hidden // WIDE,), name="feed_back",
        in_specs=[pl.BlockSpec((tokens, width), lambda j: (0, 0)), pl.BlockSpec((WIDE, width), lambda j: (j % halves, j // halves)), tile],
        out_specs=[tile, pl.BlockSpec((1, WIDE), lambda j: (0, j))],
        out_shape=[jax.ShapeDtypeStruct((tokens, hidden), BF), jax.ShapeDtypeStruct((1, hidden), F32)], compiler_params=PARAMS)(dz, weight, slope)


def settle_kernel(
    hidden_ref, w_ref, bias_ref, first_ref, gain_ref, shift_ref, cot_ref,
    out_ref, grad_ref, low_ref, gain_sum, shift_sum, bias_sum,
):
    width = first_ref.shape[1]
    gain = gain_ref[...]
    total = first_ref[...] + bias_ref[...]
    for block in range(hidden_ref.shape[1] // width):
        at = slice(block * width, (block + 1) * width)
        total += matmul(hidden_ref[:, at], w_ref[:, at])
    output, normed, inverse = normalize(total, gain, shift_ref[...])
    out_ref[...] = output.astype(BF)
    incoming = cot_ref[...].astype(F32)
    scaled = incoming * gain
    inner = scaled - jnp.mean(scaled, axis=-1, keepdims=True)
    inner = inner - normed * jnp.mean(scaled * normed, axis=-1, keepdims=True)
    grad = inverse * inner
    low = grad.astype(BF)
    grad_ref[...] = grad
    low_ref[...] = low

    @pl.when(pl.program_id(0) == 0)
    def _():
        for ref in (gain_sum, shift_sum, bias_sum):
            ref[...] = jnp.zeros(ref.shape, F32)

    gain_sum[...] += jnp.sum(incoming * normed, axis=0, keepdims=True)
    shift_sum[...] += jnp.sum(incoming, axis=0, keepdims=True)
    bias_sum[...] += jnp.sum(low.astype(F32), axis=0, keepdims=True)


def settle(hidden, packed, bias, first, gain, shift, cotangent):
    tokens, width = first.shape
    units = hidden.shape[1]
    row = pl.BlockSpec((TILE, width), lambda i: (i, 0))
    vector = pl.BlockSpec((1, width), lambda i: (0, 0))
    return pl.pallas_call(
        settle_kernel,
        grid=(tokens // TILE,),
        name="settle",
        in_specs=[
            pl.BlockSpec((TILE, units), lambda i: (i, 0)),
            pl.BlockSpec((width, units), lambda i: (0, 0)),
            vector, row, vector, vector, row,
        ],
        out_specs=[row, row, row, vector, vector, vector],
        out_shape=[
            jax.ShapeDtypeStruct((tokens, width), BF),
            jax.ShapeDtypeStruct((tokens, width), F32),
            jax.ShapeDtypeStruct((tokens, width), BF),
        ]
        + [jax.ShapeDtypeStruct((1, width), F32)] * 3,
        compiler_params=PARAMS,
    )(hidden, packed, bias.reshape(1, -1), first, gain.reshape(1, -1), shift.reshape(1, -1), cotangent)


def weight_kernel(own_ref, rows_t_ref, part_ref, keep_ref, send_ref):
    share, step = keep_ref.shape[1:]
    grad = matmul(rows_t_ref[...], part_ref[0]).astype(BF).reshape(-1, 2, share, step)

    @pl.when(own_ref[0] == 0)
    def _():
        keep_ref[...] = grad[:, 0]
        send_ref[...] = grad[:, 1]

    @pl.when(own_ref[0] == 1)
    def _():
        keep_ref[...] = grad[:, 1]
        send_ref[...] = grad[:, 0]


def weight_halves(rows_t, parts, devices):
    (width, tokens), step = rows_t.shape, parts.shape[2]
    own = (lax.axis_index(AXES) & 1).astype(jnp.int32).reshape(1)
    half = (devices // 2, width // devices)
    spec = pl.BlockSpec(half + (step,), lambda i: (0, 0, i))
    return pl.pallas_call(
        weight_kernel,
        grid=(3,),
        name="weight_halves",
        in_specs=[
            pl.BlockSpec(memory_space=pltpu.SMEM),
            pl.BlockSpec((width, tokens), lambda i: (0, 0)),
            pl.BlockSpec((1, tokens, step), lambda i: (i, 0, 0)),
        ],
        out_specs=[spec, spec],
        out_shape=[jax.ShapeDtypeStruct(half + (3 * step,), BF)] * 2,
        compiler_params=PARAMS,
    )(own, rows_t, parts)


def input_kernel(*refs):
    base_ref, weight_ref, pieces, out_ref = refs[0], refs[1], refs[2:-1], refs[-1]
    width = base_ref.shape[1]
    step = pieces[0].shape[2]
    total = base_ref[...]
    for i, ref in enumerate(pieces):
        for part in range(3):
            first = PAIR + part * width + i * step
            total += contract_cols(ref[part], weight_ref[:, first : first + step])
    out_ref[...] = total.astype(BF)


def input_call(base, head, pieces):
    tokens, width = base.shape
    step = pieces[0].shape[2]
    row = pl.BlockSpec((TILE, width), lambda i: (i, 0))
    return pl.pallas_call(
        input_kernel,
        grid=(tokens // TILE,),
        name="input_grad",
        in_specs=[row, pl.BlockSpec(head.shape, lambda i: (0, 0))]
        + [pl.BlockSpec((3, TILE, step), lambda i: (0, i, 0))] * len(pieces),
        out_specs=row,
        out_shape=jax.ShapeDtypeStruct((tokens, width), BF),
        compiler_params=PARAMS,
    )(base, head, *pieces)


def swap(value, bit, devices):
    return lax.ppermute(value, AXES, [(i, i ^ (1 << bit)) for i in range(devices)])


def bit_orders(bits):
    rest = list(range(1, bits))
    starts = (0, (bits - 1) // 4, (bits - 1) // 2)
    return [[0] + rest[s:] + rest[:s] for s in starts]


def spans(width, parts):
    step = width // PAIR // parts * PAIR
    edges = [step * p for p in range(parts)] + [width]
    return list(zip(edges[:-1], edges[1:]))


class Chain:
    def __init__(self, value, order, devices, kind=BF, pair=None):
        self.devices, self.kind, self.order = devices, kind, list(order)
        self.left = list(range(devices.bit_length() - 1))
        self.bits = len(self.left)
        self.lead = value.shape[:-2]
        shape = self.lead + (2,) * self.bits + (value.shape[-2] // devices, value.shape[-1])
        self.got = None
        if pair is None:
            self.halve([value.reshape(shape)])
        else:
            self.left.pop()
            self.keep, self.send = (half.reshape(shape[1:]) for half in pair)

    def halve(self, terms):
        bit = self.order[0]
        axis = len(self.lead) + self.left.index(self.bits - 1 - bit)
        own = (lax.axis_index(AXES) >> bit) & 1
        mine = [lax.dynamic_index_in_dim(t, own, axis, keepdims=False) for t in terms]
        theirs = [lax.dynamic_index_in_dim(t, 1 - own, axis, keepdims=False) for t in terms]
        self.keep = mine[0] if len(terms) == 1 else mine[0].astype(F32) + mine[1].astype(F32)
        send = theirs[0] if len(terms) == 1 else theirs[0].astype(F32) + theirs[1].astype(F32)
        self.send = send.astype(self.kind)
        self.left.pop(axis - len(self.lead))

    def begin(self):
        self.got = swap(self.send, self.order.pop(0), self.devices)

    def finish(self):
        got, self.got = self.got, None
        if self.order:
            self.halve([self.keep, got])
        else:
            self.keep, self.send = self.keep.astype(F32) + got.astype(F32), None

    @property
    def over(self):
        return self.send is None


def tick(chains, value):
    active = [c for c in chains if not c.over]
    for c in active:
        if c.got is not None:
            c.finish()
    held = lax.optimization_barrier((value, [(c.keep, c.send) for c in active]))
    for c, (keep, send) in zip(active, held[1]):
        c.keep, c.send = keep, send
        if not c.over:
            c.begin()
    return held[0]


def chains_of(value, devices, parts=3, turn=0, kind=BF):
    orders = bit_orders(devices.bit_length() - 1)
    return [
        Chain(value[:, a:b], orders[(p + turn) % 3], devices, kind)
        for p, (a, b) in enumerate(spans(value.shape[1], parts))
    ]


def result(chains):
    return jnp.concatenate([c.keep for c in chains], axis=1)


def gather_pairs(value, devices, later, parts=3):
    bits = devices.bit_length() - 1
    here = lax.axis_index(AXES)
    orders = [order[::-1] for order in bit_orders(bits)]
    work = [value[:, a:b] for a, b in spans(value.shape[1], parts)]
    held = [[] for _ in range(parts)]
    for step in range(bits):
        for p in range(parts):
            bit = orders[p][step]
            name = bits - 1 - bit
            axis = sum(1 for h in held[p] if h < name)
            own = (here >> bit) & 1
            mine, got = work[p], swap(work[p], bit, devices)
            work[p] = jnp.where(own == 0, jnp.stack([mine, got], axis), jnp.stack([got, mine], axis))
            held[p] = sorted(held[p] + [name])
        if step == bits - 3:
            work, later = lax.optimization_barrier((work, later))
    return [w.reshape(devices * value.shape[0], w.shape[-1]) for w in work], later


def widen(vector):
    return vector.astype(F32)


def local(
    tokens, segment_ids, cotangent, w_query, b_query, w_key, w_value, b_value, w_out, b_out,
    gain_attn, shift_attn, w_up, b_up, w_down, b_down, gain_ffn, shift_ffn, devices,
):
    blocks, length, width = tokens.shape
    rows = tokens.reshape(blocks * length, width)
    rows_t = rows.T
    own = w_query.shape[0]
    ratio = b_up.shape[0] // own
    vectors = [b_query, b_value, b_out, gain_attn, shift_attn, b_down, gain_ffn, shift_ffn]
    names = len(vectors)
    side = jnp.stack(vectors, axis=1)
    side = jnp.concatenate([side, b_up.reshape(own, ratio)], axis=1)
    side = jnp.pad(side, ((0, 0), (0, PAIR - names - ratio)))
    head = jnp.concatenate([side, w_query, w_key, w_value], axis=1).astype(BF)
    down_side = w_down.reshape(ratio, own, width).transpose(1, 0, 2).reshape(own, ratio * width)
    up_side = w_up.astype(BF).reshape(own, devices, ratio, own).transpose(0, 2, 1, 3)
    later = jnp.concatenate(
        [down_side.astype(BF), up_side.reshape(own, -1), w_out.astype(BF)], axis=1
    )
    head, later = gather_pairs(head, devices, later)
    head = jnp.concatenate(head, axis=1)
    packed_full = head[:, PAIR:]
    query_bias, value_bias, out_bias, attn_gain, attn_shift, down_bias, ffn_gain, ffn_shift = [
        widen(head[:, i]) for i in range(names)
    ]
    up_bias = widen(head[:, names : names + ratio].reshape(-1))
    up_bias = up_bias.reshape(devices, ratio, own).transpose(1, 0, 2).reshape(-1)
    rest = lax.all_gather(later, AXES, axis=0, tiled=True)
    units = ratio * width
    up_full, out_full = rest[:, units : 2 * units], rest[:, 2 * units :]

    packed_bias = jnp.concatenate([query_bias, jnp.zeros_like(query_bias), value_bias])
    packed = (matmul(rows, packed_full) + packed_bias).astype(BF)
    segments = segment_ids.reshape(-1)
    context, logsums = attend(segments, packed)
    attended = matmul(context, out_full) + out_bias
    first, normed_one, inverse_one = normalize(rows.astype(F32) + attended, attn_gain, attn_shift)
    first_low = first.astype(BF)
    hidden, slope = up_call(first_low, rest, up_bias)
    output, grad_two, grad_branch, ffn_gain_grad, ffn_shift_grad, down_bias_grad = settle(
        hidden, rest, down_bias, first, ffn_gain, ffn_shift, cotangent.reshape(blocks * length, width)
    )
    encoder_output = output.reshape(tokens.shape)
    ffn_gain_grad, ffn_shift_grad, down_bias_grad = ffn_gain_grad[0], ffn_shift_grad[0], down_bias_grad[0]

    down_product = contract_rows(hidden, grad_branch).astype(BF).reshape(ratio, width, width)
    orders = bit_orders(devices.bit_length() - 1)
    down = [
        Chain(down_product[p * ratio // 2 : (p + 1) * ratio // 2], orders[p], devices) for p in range(2)
    ]
    running = list(down)
    grad_branch = tick(running, grad_branch)
    grad_pre, up_bias_grad = up_back_call(grad_branch, rest, slope)
    up_bias_grad = up_bias_grad[0]
    grad_pre = tick(running, grad_pre)
    up_product = contract_rows(first_low, grad_pre).astype(BF)
    up = chains_of(up_product, devices, parts=2, turn=2)
    running += up
    grad_pre = tick(running, grad_pre)
    grad_first = grad_two + contract_cols(grad_pre, up_full)
    grad_one, attn_gain_grad, attn_shift_grad = normalize_back(
        grad_first, normed_one, inverse_one, attn_gain
    )
    grad_attended = grad_one.astype(BF)
    out_bias_grad = jnp.sum(grad_attended.astype(F32), axis=0)
    out_product = contract_rows(context, grad_attended).astype(BF)
    out = chains_of(out_product, devices, parts=1, turn=2)
    grad_context = contract_cols(grad_attended, out_full).astype(BF)
    running += out

    pieces, shares = [], []
    for chunk in range(CHUNKS):
        grad_context = tick(running, grad_context)
        piece = attend_back(segments, packed, grad_context, logsums, chunk)
        if chunk + 1 < CHUNKS:
            grad_context, piece = lax.optimization_barrier((grad_context, piece))
        pieces.append(piece)
        if own % 32 == 0:
            pair = weight_halves(rows_t, piece[0], devices)
            order = bit_orders(devices.bit_length() - 1)[chunk % 3]
            grads = jax.ShapeDtypeStruct((width, pair[0].shape[2]), BF)
            shares.append([Chain(grads, order, devices, pair=pair)])
        else:
            grads = jnp.concatenate([matmul(rows_t, piece[0][part]).astype(BF) for part in range(3)], axis=1)
            shares.append(chains_of(grads, devices, parts=1, turn=chunk))
        running += shares[-1]
    joined = [jnp.concatenate([piece[part] for piece in pieces], axis=1) for part in (1, 2)]
    vector_grads = [
        joined[0][0], joined[1][0], out_bias_grad, attn_gain_grad, attn_shift_grad,
        down_bias_grad, ffn_gain_grad, ffn_shift_grad,
    ]
    side_grad = jnp.concatenate(
        [v.reshape(devices, own) for v in vector_grads] + [up_bias_grad.reshape(ratio, devices, own).transpose(1, 0, 2).reshape(devices, -1)],
        axis=1,
    )
    side = chains_of(side_grad, devices, parts=1, kind=F32)
    running += side
    tick(running, ())
    pieces = tick(running, [piece[0] for piece in pieces])
    total_input = input_call(grad_one, head, pieces)
    layer_input_gradient = total_input.reshape(tokens.shape)
    while not all(c.over for c in running):
        tick(running, ())

    up_grad, out_grad = result(up), result(out)
    up_grad = up_grad.reshape(own, ratio, devices, own).transpose(0, 2, 1, 3).reshape(own, -1)
    down_grad = jnp.concatenate([c.keep for c in down], axis=0).reshape(ratio * own, width)
    shares = [result(share) for share in shares]
    step = width // CHUNKS
    query_grad, key_grad, value_grad = [
        jnp.concatenate([share[:, part * step : (part + 1) * step] for share in shares], axis=1)
        for part in range(3)
    ]
    side_grad = result(side)[0]
    parts = [side_grad[i * own : (i + 1) * own] for i in range(names)]
    up_bias_share = side_grad[names * own :]
    return (
        encoder_output, layer_input_gradient, query_grad, parts[0], key_grad, value_grad, parts[1],
        out_grad, parts[2], parts[3], parts[4], up_grad, up_bias_share, down_grad, parts[5],
        parts[6], parts[7],
    )


def solution(mesh):
    devices = mesh.shape["fsdp"] * mesh.shape["rep"]
    act, ids = P("rep", "fsdp", None), P("rep", "fsdp")
    mat, vec = P(AXES, None), P(AXES)
    return jax.shard_map(
        partial(local, devices=devices),
        mesh=mesh,
        in_specs=(
            act, ids, act, mat, vec, mat, mat, vec, mat, vec, vec, vec, mat, vec, mat, vec, vec, vec,
        ),
        out_specs=(act, act, mat, vec, mat, mat, vec, mat, vec, vec, vec, mat, vec, mat, vec, vec, vec),
        check_vma=False,
    )
```

```python
from functools import partial

import jax
import jax.numpy as jnp
from jax import lax
from jax.experimental import pallas as pl
from jax.experimental.pallas import tpu as pltpu
from jax.sharding import PartitionSpec as P


HEAD_DIM = 64
PAIR = 128
TILE = 256
CHUNKS = 4
SCALE = 0.125
EPS = 1e-05
NEG = -1e30
BELL = (2.0 * 3.141592653589793) ** -0.5
AXES = ("fsdp", "rep")
BF = jnp.bfloat16
F32 = jnp.float32


def matmul(left, right):
    return jnp.dot(left, right, preferred_element_type=F32)


def contract_rows(left, right):
    return lax.dot_general(left, right, (((0,), (0,)), ((), ())), preferred_element_type=F32)


def contract_cols(left, right):
    return lax.dot_general(left, right, (((1,), (1,)), ((), ())), preferred_element_type=F32)


def normalize(hidden, gain, shift):
    mean = jnp.mean(hidden, axis=-1, keepdims=True)
    centered = hidden - mean
    inverse = lax.rsqrt(jnp.mean(centered * centered, axis=-1, keepdims=True) + EPS)
    normed = centered * inverse
    return (normed * gain + shift, normed, inverse)


def normalize_back(grad, normed, inverse, gain):
    scaled = grad * gain
    inner = scaled - jnp.mean(scaled, axis=-1, keepdims=True)
    inner = inner - normed * jnp.mean(scaled * normed, axis=-1, keepdims=True)
    return (inverse * inner, jnp.sum(grad * normed, axis=0), jnp.sum(grad, axis=0))


def fill_bias(seg_col, seg_row, bias):
    @pl.when(pl.program_id(0) == 0)
    def _():
        bias[...] = jnp.where(seg_col[...] == seg_row[...], 0.0, NEG)


def head_lanes(head):
    lane = lax.broadcasted_iota(jnp.int32, (TILE, PAIR), 1)
    return lane < HEAD_DIM if head == 0 else lane >= HEAD_DIM


def forward_kernel(seg_col, seg_row, q_ref, k_ref, v_ref, o_ref, lse_ref, bias, out_t):
    fill_bias(seg_col, seg_row, bias)
    keys = k_ref[...]
    values_t = v_ref[...].T
    for tile in range(q_ref.shape[0] // TILE):
        at = slice(tile * TILE, (tile + 1) * TILE)
        query = q_ref[at, :] * jnp.asarray(SCALE, BF)
        for head in range(2):
            mine = jnp.where(head_lanes(head), query, jnp.zeros_like(query))
            scores = contract_cols(keys, mine) + bias[:, at]
            top = jnp.max(scores, axis=0, keepdims=True)
            weights = jnp.exp(scores - top)
            total = jnp.sum(weights, axis=0, keepdims=True)
            rows = slice(head * HEAD_DIM, (head + 1) * HEAD_DIM)
            out_t[rows, at] = matmul(values_t[rows, :], weights.astype(BF)) * (1.0 / total)
            lse_ref[0, head : head + 1, at] = top + jnp.log(total)
    o_ref[...] = out_t[...].T.astype(BF)


def backward_kernel(
    seg_col, seg_row, q_ref, k_ref, v_ref, do_ref, lse_ref,
    grads_ref, bq_ref, bv_ref, bias, dq_t, dk_sum, dv_sum,
):
    fill_bias(seg_col, seg_row, bias)
    keys = k_ref[...]
    values = v_ref[...]
    keys_t = keys.T
    for tile in range(q_ref.shape[0] // TILE):
        at = slice(tile * TILE, (tile + 1) * TILE)
        query = q_ref[at, :]
        grad = do_ref[at, :]
        for head in range(2):
            lanes = head_lanes(head)
            query_h = jnp.where(lanes, query, jnp.zeros_like(query))
            grad_h = jnp.where(lanes, grad, jnp.zeros_like(grad))
            scores = contract_cols(keys, query_h * jnp.asarray(SCALE, BF)) + bias[:, at]
            probs = jnp.exp(scores - lse_ref[0, head : head + 1, at])
            grad_probs = contract_cols(values, grad_h)
            inner = jnp.sum(grad_probs * probs, axis=0, keepdims=True)
            grad_scores = (probs * (grad_probs - inner)).astype(BF)
            rows = slice(head * HEAD_DIM, (head + 1) * HEAD_DIM)
            dq_t[rows, at] = matmul(keys_t[rows, :], grad_scores)
            dk_part = matmul(grad_scores, query_h)
            dv_part = matmul(probs.astype(BF), grad_h)
            if tile == 0 and head == 0:
                dk_sum[...] = dk_part
                dv_sum[...] = dv_part
            else:
                dk_sum[...] += dk_part
                dv_sum[...] += dv_part
    dq = (dq_t[...].T * SCALE).astype(BF)
    dv = dv_sum[...].astype(BF)
    grads_ref[0] = dq
    grads_ref[1] = (dk_sum[...] * SCALE).astype(BF)
    grads_ref[2] = dv
    bq_ref[...] = jnp.sum(dq.astype(F32), axis=0, keepdims=True)
    bv_ref[...] = jnp.sum(dv.astype(F32), axis=0, keepdims=True)


def columns(tokens, first):
    return pl.BlockSpec((tokens, PAIR), lambda i: (0, first + i))


def segment_specs(tokens):
    return [pl.BlockSpec((tokens, 1), lambda i: (0, 0)), pl.BlockSpec((1, tokens), lambda i: (0, 0))]


PARAMS = pltpu.CompilerParams(dimension_semantics=("arbitrary",), vmem_limit_bytes=56 * 2**20)


def attend(segments, packed):
    tokens = packed.shape[0]
    width = packed.shape[1] // 3
    pairs = width // PAIR
    return pl.pallas_call(
        forward_kernel,
        grid=(pairs,),
        name="attend",
        in_specs=segment_specs(tokens) + [columns(tokens, part * pairs) for part in range(3)],
        out_specs=[columns(tokens, 0), pl.BlockSpec((1, 2, tokens), lambda i: (i, 0, 0))],
        out_shape=[
            jax.ShapeDtypeStruct((tokens, width), BF),
            jax.ShapeDtypeStruct((pairs, 2, tokens), F32),
        ],
        scratch_shapes=[pltpu.VMEM((tokens, tokens), F32), pltpu.VMEM((PAIR, tokens), F32)],
        compiler_params=PARAMS,
    )(segments.reshape(tokens, 1), segments.reshape(1, tokens), packed, packed, packed)


def attend_back(segments, packed, grad, logsum, chunk):
    tokens = packed.shape[0]
    width = packed.shape[1] // 3
    pairs = width // PAIR
    count = pairs // CHUNKS
    first = chunk * count
    row = pl.BlockSpec((1, PAIR), lambda i: (0, i))
    return pl.pallas_call(
        backward_kernel,
        grid=(count,),
        name="attend_back",
        in_specs=segment_specs(tokens)
        + [columns(tokens, part * pairs + first) for part in range(3)]
        + [columns(tokens, first), pl.BlockSpec((1, 2, tokens), lambda i: (first + i, 0, 0))],
        out_specs=[pl.BlockSpec((3, tokens, PAIR), lambda i: (0, 0, i))] + [row] * 2,
        out_shape=[jax.ShapeDtypeStruct((3, tokens, count * PAIR), BF)]
        + [jax.ShapeDtypeStruct((1, count * PAIR), F32)] * 2,
        scratch_shapes=[
            pltpu.VMEM((tokens, tokens), F32),
            pltpu.VMEM((PAIR, tokens), F32),
            pltpu.VMEM((tokens, PAIR), F32),
            pltpu.VMEM((tokens, PAIR), F32),
        ],
        compiler_params=PARAMS,
    )(segments.reshape(tokens, 1), segments.reshape(1, tokens), packed, packed, packed, grad, logsum)


WIDE = 512


def natural(w_ref, out_ref, own):
    width = out_ref.shape[1]
    ratio = w_ref.shape[1] // width
    for device in range(w_ref.shape[0] // own):
        for block in range(ratio):
            row = (device * ratio + block) * own
            out_ref[row : row + own, :] = w_ref[
                device * own : (device + 1) * own, block * width : (block + 1) * width
            ]


def up_kernel(x_ref, w_ref, b_ref, hidden_ref, slope_ref):
    weight = w_ref[...]
    bias = b_ref[...]
    for tile in range(x_ref.shape[0] // TILE):
        at = slice(tile * TILE, (tile + 1) * TILE)
        pre = matmul(x_ref[at, :], weight) + bias
        area = 0.5 * lax.erf(pre * (0.5 ** 0.5)) + 0.5
        hidden_ref[at, :] = (pre * area).astype(BF)
        bell = jnp.exp(pre * pre * -0.5) * BELL
        slope_ref[at, :] = (area + pre * bell).astype(BF)


def up_back_kernel(dz_ref, w_ref, slope_ref, du_ref, sum_ref, weight_ref, own):
    natural(w_ref, weight_ref, own)
    weight = weight_ref[...]
    total = jnp.zeros(sum_ref.shape, F32)
    for tile in range(dz_ref.shape[0] // TILE):
        at = slice(tile * TILE, (tile + 1) * TILE)
        du = (contract_cols(dz_ref[at, :], weight) * slope_ref[at, :].astype(F32)).astype(BF)
        du_ref[at, :] = du
        total += jnp.sum(du.astype(F32), axis=0, keepdims=True)
    sum_ref[...] = total


def up_call(x, packed, bias):
    tokens, width = x.shape
    hidden = bias.shape[0]
    tile = pl.BlockSpec((tokens, WIDE), lambda j: (0, j))
    return pl.pallas_call(up_kernel, grid=(hidden // WIDE,), name="feed",
        in_specs=[pl.BlockSpec((tokens, width), lambda j: (0, 0)),
                  pl.BlockSpec((width, WIDE), lambda j: (0, hidden // WIDE + j)),
                  pl.BlockSpec((1, WIDE), lambda j: (0, j))],
        out_specs=[tile, tile],
        out_shape=[jax.ShapeDtypeStruct((tokens, hidden), BF)] * 2, compiler_params=PARAMS)(x, packed, bias.reshape(1, hidden))


def up_back_call(dz, weight, slope, own):
    tokens, width = dz.shape
    hidden = slope.shape[1]
    sides = hidden // width
    tile = pl.BlockSpec((tokens, WIDE), lambda j: (0, j))
    return pl.pallas_call(partial(up_back_kernel, own=own), scratch_shapes=[pltpu.VMEM((WIDE, width), BF)], grid=(hidden // WIDE,), name="feed_back",
        in_specs=[pl.BlockSpec((tokens, width), lambda j: (0, 0)), pl.BlockSpec((WIDE // sides, hidden), lambda j: (j, 0)), tile],
        out_specs=[tile, pl.BlockSpec((1, WIDE), lambda j: (0, j))],
        out_shape=[jax.ShapeDtypeStruct((tokens, hidden), BF), jax.ShapeDtypeStruct((1, hidden), F32)], compiler_params=PARAMS)(dz, weight, slope)


def settle_kernel(
    hidden_ref, w_ref, bias_ref, first_ref, gain_ref, shift_ref, cot_ref,
    out_ref, grad_ref, low_ref, gain_sum, shift_sum, bias_sum, weight_ref, own,
):
    gain = gain_ref[...]

    @pl.when(pl.program_id(0) == 0)
    def _():
        natural(w_ref, weight_ref, own)

    total = first_ref[...] + bias_ref[...] + matmul(hidden_ref[...], weight_ref[...])
    output, normed, inverse = normalize(total, gain, shift_ref[...])
    out_ref[...] = output.astype(BF)
    incoming = cot_ref[...].astype(F32)
    scaled = incoming * gain
    inner = scaled - jnp.mean(scaled, axis=-1, keepdims=True)
    inner = inner - normed * jnp.mean(scaled * normed, axis=-1, keepdims=True)
    grad = inverse * inner
    low = grad.astype(BF)
    grad_ref[...] = grad
    low_ref[...] = low

    @pl.when(pl.program_id(0) == 0)
    def _():
        for ref in (gain_sum, shift_sum, bias_sum):
            ref[...] = jnp.zeros(ref.shape, F32)

    gain_sum[...] += jnp.sum(incoming * normed, axis=0, keepdims=True)
    shift_sum[...] += jnp.sum(incoming, axis=0, keepdims=True)
    bias_sum[...] += jnp.sum(low.astype(F32), axis=0, keepdims=True)


def settle(hidden, packed, bias, first, gain, shift, cotangent, own):
    tokens, width = first.shape
    units = hidden.shape[1]
    row = pl.BlockSpec((TILE, width), lambda i: (i, 0))
    vector = pl.BlockSpec((1, width), lambda i: (0, 0))
    return pl.pallas_call(
        partial(settle_kernel, own=own),
        scratch_shapes=[pltpu.VMEM((units, width), BF)],
        grid=(tokens // TILE,),
        name="settle",
        in_specs=[
            pl.BlockSpec((TILE, units), lambda i: (i, 0)),
            pl.BlockSpec((width, units), lambda i: (0, 0)),
            vector, row, vector, vector, row,
        ],
        out_specs=[row, row, row, vector, vector, vector],
        out_shape=[
            jax.ShapeDtypeStruct((tokens, width), BF),
            jax.ShapeDtypeStruct((tokens, width), F32),
            jax.ShapeDtypeStruct((tokens, width), BF),
        ]
        + [jax.ShapeDtypeStruct((1, width), F32)] * 3,
        compiler_params=PARAMS,
    )(hidden, packed, bias.reshape(1, -1), first, gain.reshape(1, -1), shift.reshape(1, -1), cotangent)


def weight_kernel(own_ref, rows_t_ref, part_ref, keep_ref, send_ref):
    share, step = keep_ref.shape[1:]
    grad = matmul(rows_t_ref[...], part_ref[0]).astype(BF).reshape(-1, 2, share, step)

    @pl.when(own_ref[0] == 0)
    def _():
        keep_ref[...] = grad[:, 0]
        send_ref[...] = grad[:, 1]

    @pl.when(own_ref[0] == 1)
    def _():
        keep_ref[...] = grad[:, 1]
        send_ref[...] = grad[:, 0]


def weight_halves(rows_t, parts, devices):
    (width, tokens), step = rows_t.shape, parts.shape[2]
    own = (lax.axis_index(AXES) & 1).astype(jnp.int32).reshape(1)
    half = (devices // 2, width // devices)
    spec = pl.BlockSpec(half + (step,), lambda i: (0, 0, i))
    return pl.pallas_call(
        weight_kernel,
        grid=(3,),
        name="weight_halves",
        in_specs=[
            pl.BlockSpec(memory_space=pltpu.SMEM),
            pl.BlockSpec((width, tokens), lambda i: (0, 0)),
            pl.BlockSpec((1, tokens, step), lambda i: (i, 0, 0)),
        ],
        out_specs=[spec, spec],
        out_shape=[jax.ShapeDtypeStruct(half + (3 * step,), BF)] * 2,
        compiler_params=PARAMS,
    )(own, rows_t, parts)


def input_kernel(*refs):
    base_ref, weight_ref, pieces, out_ref = refs[0], refs[1], refs[2:-1], refs[-1]
    width = base_ref.shape[1]
    step = pieces[0].shape[2]
    total = base_ref[...]
    for i, ref in enumerate(pieces):
        for part in range(3):
            first = PAIR + part * width + i * step
            total += contract_cols(ref[part], weight_ref[:, first : first + step])
    out_ref[...] = total.astype(BF)


def input_call(base, head, pieces):
    tokens, width = base.shape
    step = pieces[0].shape[2]
    row = pl.BlockSpec((TILE, width), lambda i: (i, 0))
    return pl.pallas_call(
        input_kernel,
        grid=(tokens // TILE,),
        name="input_grad",
        in_specs=[row, pl.BlockSpec(head.shape, lambda i: (0, 0))]
        + [pl.BlockSpec((3, TILE, step), lambda i: (0, i, 0))] * len(pieces),
        out_specs=row,
        out_shape=jax.ShapeDtypeStruct((tokens, width), BF),
        compiler_params=PARAMS,
    )(base, head, *pieces)


def swap(value, bit, devices):
    return lax.ppermute(value, AXES, [(i, i ^ (1 << bit)) for i in range(devices)])


def bit_orders(bits):
    rest = list(range(1, bits))
    starts = (0, (bits - 1) // 4, (bits - 1) // 2)
    return [[0] + rest[s:] + rest[:s] for s in starts]


def spans(width, parts):
    step = width // PAIR // parts * PAIR
    edges = [step * p for p in range(parts)] + [width]
    return list(zip(edges[:-1], edges[1:]))


class Chain:
    def __init__(self, value, order, devices, kind=BF, pair=None):
        self.devices, self.kind, self.order = devices, kind, list(order)
        self.left = list(range(devices.bit_length() - 1))
        self.bits = len(self.left)
        self.lead = value.shape[:-2]
        shape = self.lead + (2,) * self.bits + (value.shape[-2] // devices, value.shape[-1])
        self.got = None
        if pair is None:
            self.halve([value.reshape(shape)])
        else:
            self.left.pop()
            self.keep, self.send = (half.reshape(shape[1:]) for half in pair)

    def halve(self, terms):
        bit = self.order[0]
        axis = len(self.lead) + self.left.index(self.bits - 1 - bit)
        own = (lax.axis_index(AXES) >> bit) & 1
        mine = [lax.dynamic_index_in_dim(t, own, axis, keepdims=False) for t in terms]
        theirs = [lax.dynamic_index_in_dim(t, 1 - own, axis, keepdims=False) for t in terms]
        self.keep = mine[0] if len(terms) == 1 else mine[0].astype(F32) + mine[1].astype(F32)
        send = theirs[0] if len(terms) == 1 else theirs[0].astype(F32) + theirs[1].astype(F32)
        self.send = send.astype(self.kind)
        self.left.pop(axis - len(self.lead))

    def begin(self):
        self.got = swap(self.send, self.order.pop(0), self.devices)

    def finish(self):
        got, self.got = self.got, None
        if self.order:
            self.halve([self.keep, got])
        else:
            self.keep, self.send = self.keep.astype(F32) + got.astype(F32), None

    @property
    def over(self):
        return self.send is None


def tick(chains, value):
    active = [c for c in chains if not c.over]
    for c in active:
        if c.got is not None:
            c.finish()
    held = lax.optimization_barrier((value, [(c.keep, c.send) for c in active]))
    for c, (keep, send) in zip(active, held[1]):
        c.keep, c.send = keep, send
        if not c.over:
            c.begin()
    return held[0]


def chains_of(value, devices, parts=3, turn=0, kind=BF):
    orders = bit_orders(devices.bit_length() - 1)
    return [
        Chain(value[:, a:b], orders[(p + turn) % 3], devices, kind)
        for p, (a, b) in enumerate(spans(value.shape[1], parts))
    ]


def result(chains):
    return jnp.concatenate([c.keep for c in chains], axis=1)


def gather_pairs(value, devices, later, parts=3):
    bits = devices.bit_length() - 1
    here = lax.axis_index(AXES)
    orders = [order[::-1] for order in bit_orders(bits)]
    work = [value[:, a:b] for a, b in spans(value.shape[1], parts)]
    held = [[] for _ in range(parts)]
    for step in range(bits):
        for p in range(parts):
            bit = orders[p][step]
            name = bits - 1 - bit
            axis = sum(1 for h in held[p] if h < name)
            own = (here >> bit) & 1
            mine, got = work[p], swap(work[p], bit, devices)
            work[p] = jnp.where(own == 0, jnp.stack([mine, got], axis), jnp.stack([got, mine], axis))
            held[p] = sorted(held[p] + [name])
        if step == bits - 3:
            work, later = lax.optimization_barrier((work, later))
    return [w.reshape(devices * value.shape[0], w.shape[-1]) for w in work], later


def widen(vector):
    return vector.astype(F32)


def local(
    tokens, segment_ids, cotangent, w_query, b_query, w_key, w_value, b_value, w_out, b_out,
    gain_attn, shift_attn, w_up, b_up, w_down, b_down, gain_ffn, shift_ffn, devices,
):
    blocks, length, width = tokens.shape
    rows = tokens.reshape(blocks * length, width)
    rows_t = rows.T
    own = w_query.shape[0]
    ratio = b_up.shape[0] // own
    vectors = [b_query, b_value, b_out, gain_attn, shift_attn, b_down, gain_ffn, shift_ffn]
    names = len(vectors)
    side = jnp.stack(vectors, axis=1)
    side = jnp.concatenate([side, b_up.reshape(own, ratio)], axis=1)
    side = jnp.pad(side, ((0, 0), (0, PAIR - names - ratio)))
    head = jnp.concatenate([side, w_query, w_key, w_value], axis=1).astype(BF)
    down_side = w_down.reshape(ratio, own, width).transpose(1, 0, 2).reshape(own, ratio * width)
    later = jnp.concatenate([down_side, w_up, w_out], axis=1).astype(BF)
    head, (later, rows_t) = gather_pairs(head, devices, (later, rows_t))
    head = jnp.concatenate(head, axis=1)
    packed_full = head[:, PAIR:]
    query_bias, value_bias, out_bias, attn_gain, attn_shift, down_bias, ffn_gain, ffn_shift = [
        widen(head[:, i]) for i in range(names)
    ]
    up_bias = widen(head[:, names : names + ratio].reshape(-1))
    rest = lax.all_gather(later, AXES, axis=0, tiled=True)
    units = ratio * width
    up_full, out_full = rest[:, units : 2 * units], rest[:, 2 * units :]
    down_rows, own_rows = rest, own
    if own % 32:
        own_rows = 32
        down_rows = rest[:, :units].reshape(devices, own, ratio, width).transpose(0, 2, 1, 3)
        down_rows = down_rows.reshape(-1, ratio, own_rows, width).transpose(0, 2, 1, 3).reshape(width, units)

    packed_bias = jnp.concatenate([query_bias, jnp.zeros_like(query_bias), value_bias])
    packed = (matmul(rows, packed_full) + packed_bias).astype(BF)
    segments = segment_ids.reshape(-1)
    context, logsums = attend(segments, packed)
    attended = matmul(context, out_full) + out_bias
    first, normed_one, inverse_one = normalize(rows.astype(F32) + attended, attn_gain, attn_shift)
    first_low = first.astype(BF)
    hidden, slope = up_call(first_low, rest, up_bias)
    output, grad_two, grad_branch, ffn_gain_grad, ffn_shift_grad, down_bias_grad = settle(
        hidden, down_rows, down_bias, first, ffn_gain, ffn_shift,
        cotangent.reshape(blocks * length, width), own_rows,
    )
    encoder_output = output.reshape(tokens.shape)
    ffn_gain_grad, ffn_shift_grad, down_bias_grad = ffn_gain_grad[0], ffn_shift_grad[0], down_bias_grad[0]

    down = chains_of(contract_rows(hidden, grad_branch).astype(BF), devices, parts=2)
    running = list(down)
    grad_branch = tick(running, grad_branch)
    grad_pre, up_bias_grad = up_back_call(grad_branch, down_rows, slope, own_rows)
    up_bias_grad = up_bias_grad[0]
    grad_pre = tick(running, grad_pre)
    up_product = contract_rows(first_low, grad_pre).astype(BF)
    up = chains_of(up_product, devices, parts=2, turn=2)
    running += up
    grad_pre = tick(running, grad_pre)
    grad_first = grad_two + contract_cols(grad_pre, up_full)
    grad_one, attn_gain_grad, attn_shift_grad = normalize_back(
        grad_first, normed_one, inverse_one, attn_gain
    )
    grad_attended = grad_one.astype(BF)
    out_bias_grad = jnp.sum(grad_attended.astype(F32), axis=0)
    out_product = contract_rows(context, grad_attended).astype(BF)
    out = chains_of(out_product, devices, parts=1, turn=2)
    grad_context = contract_cols(grad_attended, out_full).astype(BF)
    running += out

    pieces, shares = [], []
    for chunk in range(CHUNKS):
        grad_context = tick(running, grad_context)
        piece = attend_back(segments, packed, grad_context, logsums, chunk)
        if chunk + 1 < CHUNKS:
            grad_context, piece = lax.optimization_barrier((grad_context, piece))
        pieces.append(piece)
        if own % 32 == 0:
            pair = weight_halves(rows_t, piece[0], devices)
            order = bit_orders(devices.bit_length() - 1)[chunk % 3]
            grads = jax.ShapeDtypeStruct((width, pair[0].shape[2]), BF)
            shares.append([Chain(grads, order, devices, pair=pair)])
        else:
            grads = jnp.concatenate([matmul(rows_t, piece[0][part]).astype(BF) for part in range(3)], axis=1)
            shares.append(chains_of(grads, devices, parts=1, turn=chunk))
        running += shares[-1]
    joined = [jnp.concatenate([piece[part] for piece in pieces], axis=1) for part in (1, 2)]
    vector_grads = [
        joined[0][0], joined[1][0], out_bias_grad, attn_gain_grad, attn_shift_grad,
        down_bias_grad, ffn_gain_grad, ffn_shift_grad,
    ]
    side_grad = jnp.concatenate(
        [v.reshape(devices, own) for v in vector_grads] + [up_bias_grad.reshape(devices, own * ratio)],
        axis=1,
    )
    side = chains_of(side_grad, devices, parts=1, kind=F32)
    running += side
    tick(running, ())
    pieces = tick(running, [piece[0] for piece in pieces])
    total_input = input_call(grad_one, head, pieces)
    layer_input_gradient = total_input.reshape(tokens.shape)
    while not all(c.over for c in running):
        tick(running, ())

    down_grad, up_grad, out_grad = result(down), result(up), result(out)
    shares = [result(share) for share in shares]
    step = width // CHUNKS
    query_grad, key_grad, value_grad = [
        jnp.concatenate([share[:, part * step : (part + 1) * step] for share in shares], axis=1)
        for part in range(3)
    ]
    side_grad = result(side)[0]
    parts = [side_grad[i * own : (i + 1) * own] for i in range(names)]
    up_bias_share = side_grad[names * own :]
    return (
        encoder_output, layer_input_gradient, query_grad, parts[0], key_grad, value_grad, parts[1],
        out_grad, parts[2], parts[3], parts[4], up_grad, up_bias_share, down_grad, parts[5],
        parts[6], parts[7],
    )


def solution(mesh):
    devices = mesh.shape["fsdp"] * mesh.shape["rep"]
    act, ids = P("rep", "fsdp", None), P("rep", "fsdp")
    mat, vec = P(AXES, None), P(AXES)
    return jax.shard_map(
        partial(local, devices=devices),
        mesh=mesh,
        in_specs=(
            act, ids, act, mat, vec, mat, mat, vec, mat, vec, vec, vec, mat, vec, mat, vec, vec, vec,
        ),
        out_specs=(act, act, mat, vec, mat, mat, vec, mat, vec, vec, vec, mat, vec, mat, vec, vec, vec),
        check_vma=False,
    )
```

```python
from functools import partial

import jax
import jax.numpy as jnp
from jax import lax
from jax.experimental import pallas as pl
from jax.experimental.pallas import tpu as pltpu
from jax.sharding import PartitionSpec as P


HEAD_DIM = 64
PAIR = 128
TILE = 256
CHUNKS = 4
SCALE = 0.125
EPS = 1e-05
NEG = -1e30
BELL = (2.0 * 3.141592653589793) ** -0.5
AXES = ("fsdp", "rep")
BF = jnp.bfloat16
F32 = jnp.float32


def matmul(left, right):
    return jnp.dot(left, right, preferred_element_type=F32)


def contract_rows(left, right):
    return lax.dot_general(left, right, (((0,), (0,)), ((), ())), preferred_element_type=F32)


def contract_cols(left, right):
    return lax.dot_general(left, right, (((1,), (1,)), ((), ())), preferred_element_type=F32)


def normalize(hidden, gain, shift):
    mean = jnp.mean(hidden, axis=-1, keepdims=True)
    centered = hidden - mean
    inverse = lax.rsqrt(jnp.mean(centered * centered, axis=-1, keepdims=True) + EPS)
    normed = centered * inverse
    return (normed * gain + shift, normed, inverse)


def normalize_back(grad, normed, inverse, gain):
    scaled = grad * gain
    inner = scaled - jnp.mean(scaled, axis=-1, keepdims=True)
    inner = inner - normed * jnp.mean(scaled * normed, axis=-1, keepdims=True)
    return (inverse * inner, jnp.sum(grad * normed, axis=0), jnp.sum(grad, axis=0))


def fill_bias(seg_col, seg_row, bias):
    @pl.when(pl.program_id(0) == 0)
    def _():
        bias[...] = jnp.where(seg_col[...] == seg_row[...], 0.0, NEG)


def head_lanes(head):
    lane = lax.broadcasted_iota(jnp.int32, (TILE, PAIR), 1)
    return lane < HEAD_DIM if head == 0 else lane >= HEAD_DIM


def forward_kernel(seg_col, seg_row, q_ref, k_ref, v_ref, o_ref, lse_ref, bias, out_t):
    fill_bias(seg_col, seg_row, bias)
    keys = k_ref[...]
    values_t = v_ref[...].T
    for tile in range(q_ref.shape[0] // TILE):
        at = slice(tile * TILE, (tile + 1) * TILE)
        query = q_ref[at, :] * jnp.asarray(SCALE, BF)
        for head in range(2):
            mine = jnp.where(head_lanes(head), query, jnp.zeros_like(query))
            scores = contract_cols(keys, mine) + bias[:, at]
            top = jnp.max(scores, axis=0, keepdims=True)
            weights = jnp.exp(scores - top)
            total = jnp.sum(weights, axis=0, keepdims=True)
            rows = slice(head * HEAD_DIM, (head + 1) * HEAD_DIM)
            out_t[rows, at] = matmul(values_t[rows, :], weights.astype(BF)) * (1.0 / total)
            lse_ref[0, head : head + 1, at] = top + jnp.log(total)
    o_ref[...] = out_t[...].T.astype(BF)


def backward_kernel(
    seg_col, seg_row, q_ref, k_ref, v_ref, do_ref, lse_ref,
    grads_ref, bq_ref, bv_ref, bias, dq_t, dk_sum, dv_sum,
):
    fill_bias(seg_col, seg_row, bias)
    keys = k_ref[...]
    values = v_ref[...]
    keys_t = keys.T
    for tile in range(q_ref.shape[0] // TILE):
        at = slice(tile * TILE, (tile + 1) * TILE)
        query = q_ref[at, :]
        grad = do_ref[at, :]
        for head in range(2):
            lanes = head_lanes(head)
            query_h = jnp.where(lanes, query, jnp.zeros_like(query))
            grad_h = jnp.where(lanes, grad, jnp.zeros_like(grad))
            scores = contract_cols(keys, query_h * jnp.asarray(SCALE, BF)) + bias[:, at]
            probs = jnp.exp(scores - lse_ref[0, head : head + 1, at])
            grad_probs = contract_cols(values, grad_h)
            inner = jnp.sum(grad_probs * probs, axis=0, keepdims=True)
            grad_scores = (probs * (grad_probs - inner)).astype(BF)
            rows = slice(head * HEAD_DIM, (head + 1) * HEAD_DIM)
            dq_t[rows, at] = matmul(keys_t[rows, :], grad_scores)
            dk_part = matmul(grad_scores, query_h)
            dv_part = matmul(probs.astype(BF), grad_h)
            if tile == 0 and head == 0:
                dk_sum[...] = dk_part
                dv_sum[...] = dv_part
            else:
                dk_sum[...] += dk_part
                dv_sum[...] += dv_part
    dq = (dq_t[...].T * SCALE).astype(BF)
    dv = dv_sum[...].astype(BF)
    grads_ref[0] = dq
    grads_ref[1] = (dk_sum[...] * SCALE).astype(BF)
    grads_ref[2] = dv
    bq_ref[...] = jnp.sum(dq.astype(F32), axis=0, keepdims=True)
    bv_ref[...] = jnp.sum(dv.astype(F32), axis=0, keepdims=True)


def columns(tokens, first):
    return pl.BlockSpec((tokens, PAIR), lambda i: (0, first + i))


def segment_specs(tokens):
    return [pl.BlockSpec((tokens, 1), lambda i: (0, 0)), pl.BlockSpec((1, tokens), lambda i: (0, 0))]


PARAMS = pltpu.CompilerParams(dimension_semantics=("arbitrary",), vmem_limit_bytes=56 * 2**20)


def turn_kernel(x_ref, out_ref):
    out_ref[...] = x_ref[...].T


def turned(rows):
    tokens, width = rows.shape
    return pl.pallas_call(
        turn_kernel,
        grid=(tokens // TILE,),
        name="turned",
        in_specs=[pl.BlockSpec((TILE, width), lambda i: (i, 0))],
        out_specs=pl.BlockSpec((width, TILE), lambda i: (0, i)),
        out_shape=jax.ShapeDtypeStruct((width, tokens), rows.dtype),
        compiler_params=PARAMS,
    )(rows)


def project_kernel(own_ref, rows_ref, *refs):
    halves, bias_ref, out_ref, weight_ref = refs[:6], refs[6], refs[7], refs[8]
    groups, share, width = halves[0].shape

    @pl.when(pl.program_id(0) == 0)
    def _():
        for part in range(3):
            for side in range(2):
                place = own_ref[0] if side == 0 else 1 - own_ref[0]
                for group in range(groups):
                    row = pl.multiple_of((group * 2 + place) * share, share)
                    weight_ref[pl.ds(row, share), part * width : (part + 1) * width] = halves[
                        part * 2 + side
                    ][group]

    out_ref[...] = (matmul(rows_ref[...], weight_ref[...]) + bias_ref[...]).astype(BF)


def project(rows, halves, bias):
    tokens, width = rows.shape
    own = (lax.axis_index(AXES) & 1).astype(jnp.int32).reshape(1)
    flat = [half for pair in halves for half in pair]
    whole = pl.BlockSpec(flat[0].shape, lambda i: (0, 0, 0))
    return pl.pallas_call(
        project_kernel,
        grid=(tokens // TILE,),
        name="project",
        in_specs=[pl.BlockSpec(memory_space=pltpu.SMEM), pl.BlockSpec((TILE, width), lambda i: (i, 0))]
        + [whole] * 6
        + [pl.BlockSpec((1, 3 * width), lambda i: (0, 0))],
        out_specs=[
            pl.BlockSpec((TILE, 3 * width), lambda i: (i, 0)),
            pl.BlockSpec((width, 3 * width), lambda i: (0, 0)),
        ],
        out_shape=[
            jax.ShapeDtypeStruct((tokens, 3 * width), BF),
            jax.ShapeDtypeStruct((width, 3 * width), BF),
        ],
        compiler_params=PARAMS,
    )(own, rows, *flat, bias.reshape(1, -1))


def attend(segments, packed):
    tokens = packed.shape[0]
    width = packed.shape[1] // 3
    pairs = width // PAIR
    return pl.pallas_call(
        forward_kernel,
        grid=(pairs,),
        name="attend",
        in_specs=segment_specs(tokens) + [columns(tokens, part * pairs) for part in range(3)],
        out_specs=[columns(tokens, 0), pl.BlockSpec((1, 2, tokens), lambda i: (i, 0, 0))],
        out_shape=[
            jax.ShapeDtypeStruct((tokens, width), BF),
            jax.ShapeDtypeStruct((pairs, 2, tokens), F32),
        ],
        scratch_shapes=[pltpu.VMEM((tokens, tokens), F32), pltpu.VMEM((PAIR, tokens), F32)],
        compiler_params=PARAMS,
    )(segments.reshape(tokens, 1), segments.reshape(1, tokens), packed, packed, packed)


def attend_back(segments, packed, grad, logsum, chunk):
    tokens = packed.shape[0]
    width = packed.shape[1] // 3
    pairs = width // PAIR
    count = pairs // CHUNKS
    first = chunk * count
    row = pl.BlockSpec((1, PAIR), lambda i: (0, i))
    return pl.pallas_call(
        backward_kernel,
        grid=(count,),
        name="attend_back",
        in_specs=segment_specs(tokens)
        + [columns(tokens, part * pairs + first) for part in range(3)]
        + [columns(tokens, first), pl.BlockSpec((1, 2, tokens), lambda i: (first + i, 0, 0))],
        out_specs=[pl.BlockSpec((3, tokens, PAIR), lambda i: (0, 0, i))] + [row] * 2,
        out_shape=[jax.ShapeDtypeStruct((3, tokens, count * PAIR), BF)]
        + [jax.ShapeDtypeStruct((1, count * PAIR), F32)] * 2,
        scratch_shapes=[
            pltpu.VMEM((tokens, tokens), F32),
            pltpu.VMEM((PAIR, tokens), F32),
            pltpu.VMEM((tokens, PAIR), F32),
            pltpu.VMEM((tokens, PAIR), F32),
        ],
        compiler_params=PARAMS,
    )(segments.reshape(tokens, 1), segments.reshape(1, tokens), packed, packed, packed, grad, logsum)


WIDE = 512


def natural(w_ref, out_ref, own):
    width = out_ref.shape[1]
    ratio = w_ref.shape[1] // width
    for device in range(w_ref.shape[0] // own):
        for block in range(ratio):
            row = (device * ratio + block) * own
            out_ref[row : row + own, :] = w_ref[
                device * own : (device + 1) * own, block * width : (block + 1) * width
            ]


def up_kernel(x_ref, w_ref, b_ref, hidden_ref, slope_ref):
    weight = w_ref[...]
    bias = b_ref[...]
    for tile in range(x_ref.shape[0] // TILE):
        at = slice(tile * TILE, (tile + 1) * TILE)
        pre = matmul(x_ref[at, :], weight) + bias
        area = 0.5 * lax.erf(pre * (0.5 ** 0.5)) + 0.5
        hidden_ref[at, :] = (pre * area).astype(BF)
        bell = jnp.exp(pre * pre * -0.5) * BELL
        slope_ref[at, :] = (area + pre * bell).astype(BF)


def up_back_kernel(dz_ref, w_ref, slope_ref, du_ref, sum_ref, weight_ref, own):
    natural(w_ref, weight_ref, own)
    weight = weight_ref[...]
    total = jnp.zeros(sum_ref.shape, F32)
    for tile in range(dz_ref.shape[0] // TILE):
        at = slice(tile * TILE, (tile + 1) * TILE)
        du = (contract_cols(dz_ref[at, :], weight) * slope_ref[at, :].astype(F32)).astype(BF)
        du_ref[at, :] = du
        total += jnp.sum(du.astype(F32), axis=0, keepdims=True)
    sum_ref[...] = total


def up_call(x, packed, bias):
    tokens, width = x.shape
    hidden = bias.shape[0]
    tile = pl.BlockSpec((tokens, WIDE), lambda j: (0, j))
    return pl.pallas_call(up_kernel, grid=(hidden // WIDE,), name="feed",
        in_specs=[pl.BlockSpec((tokens, width), lambda j: (0, 0)),
                  pl.BlockSpec((width, WIDE), lambda j: (0, hidden // WIDE + j)),
                  pl.BlockSpec((1, WIDE), lambda j: (0, j))],
        out_specs=[tile, tile],
        out_shape=[jax.ShapeDtypeStruct((tokens, hidden), BF)] * 2, compiler_params=PARAMS)(x, packed, bias.reshape(1, hidden))


def up_back_call(dz, weight, slope, own):
    tokens, width = dz.shape
    hidden = slope.shape[1]
    sides = hidden // width
    tile = pl.BlockSpec((tokens, WIDE), lambda j: (0, j))
    return pl.pallas_call(partial(up_back_kernel, own=own), scratch_shapes=[pltpu.VMEM((WIDE, width), BF)], grid=(hidden // WIDE,), name="feed_back",
        in_specs=[pl.BlockSpec((tokens, width), lambda j: (0, 0)), pl.BlockSpec((WIDE // sides, hidden), lambda j: (j, 0)), tile],
        out_specs=[tile, pl.BlockSpec((1, WIDE), lambda j: (0, j))],
        out_shape=[jax.ShapeDtypeStruct((tokens, hidden), BF), jax.ShapeDtypeStruct((1, hidden), F32)], compiler_params=PARAMS)(dz, weight, slope)


def settle_kernel(
    hidden_ref, w_ref, bias_ref, first_ref, gain_ref, shift_ref, cot_ref,
    out_ref, grad_ref, low_ref, gain_sum, shift_sum, bias_sum, weight_ref, own,
):
    gain = gain_ref[...]

    @pl.when(pl.program_id(0) == 0)
    def _():
        natural(w_ref, weight_ref, own)

    total = first_ref[...] + bias_ref[...] + matmul(hidden_ref[...], weight_ref[...])
    output, normed, inverse = normalize(total, gain, shift_ref[...])
    out_ref[...] = output.astype(BF)
    incoming = cot_ref[...].astype(F32)
    scaled = incoming * gain
    inner = scaled - jnp.mean(scaled, axis=-1, keepdims=True)
    inner = inner - normed * jnp.mean(scaled * normed, axis=-1, keepdims=True)
    grad = inverse * inner
    low = grad.astype(BF)
    grad_ref[...] = grad
    low_ref[...] = low

    @pl.when(pl.program_id(0) == 0)
    def _():
        for ref in (gain_sum, shift_sum, bias_sum):
            ref[...] = jnp.zeros(ref.shape, F32)

    gain_sum[...] += jnp.sum(incoming * normed, axis=0, keepdims=True)
    shift_sum[...] += jnp.sum(incoming, axis=0, keepdims=True)
    bias_sum[...] += jnp.sum(low.astype(F32), axis=0, keepdims=True)


def settle(hidden, packed, bias, first, gain, shift, cotangent, own):
    tokens, width = first.shape
    units = hidden.shape[1]
    row = pl.BlockSpec((TILE, width), lambda i: (i, 0))
    vector = pl.BlockSpec((1, width), lambda i: (0, 0))
    return pl.pallas_call(
        partial(settle_kernel, own=own),
        scratch_shapes=[pltpu.VMEM((units, width), BF)],
        grid=(tokens // TILE,),
        name="settle",
        in_specs=[
            pl.BlockSpec((TILE, units), lambda i: (i, 0)),
            pl.BlockSpec((width, units), lambda i: (0, 0)),
            vector, row, vector, vector, row,
        ],
        out_specs=[row, row, row, vector, vector, vector],
        out_shape=[
            jax.ShapeDtypeStruct((tokens, width), BF),
            jax.ShapeDtypeStruct((tokens, width), F32),
            jax.ShapeDtypeStruct((tokens, width), BF),
        ]
        + [jax.ShapeDtypeStruct((1, width), F32)] * 3,
        compiler_params=PARAMS,
    )(hidden, packed, bias.reshape(1, -1), first, gain.reshape(1, -1), shift.reshape(1, -1), cotangent)


def weight_kernel(own_ref, rows_t_ref, part_ref, keep_ref, send_ref):
    share, step = keep_ref.shape[1:]
    grad = matmul(rows_t_ref[...], part_ref[0]).astype(BF).reshape(-1, 2, share, step)

    @pl.when(own_ref[0] == 0)
    def _():
        keep_ref[...] = grad[:, 0]
        send_ref[...] = grad[:, 1]

    @pl.when(own_ref[0] == 1)
    def _():
        keep_ref[...] = grad[:, 1]
        send_ref[...] = grad[:, 0]


def weight_halves(rows_t, parts, devices):
    (width, tokens), step = rows_t.shape, parts.shape[2]
    own = (lax.axis_index(AXES) & 1).astype(jnp.int32).reshape(1)
    half = (devices // 2, width // devices)
    spec = pl.BlockSpec(half + (step,), lambda i: (0, 0, i))
    return pl.pallas_call(
        weight_kernel,
        grid=(3,),
        name="weight_halves",
        in_specs=[
            pl.BlockSpec(memory_space=pltpu.SMEM),
            pl.BlockSpec((width, tokens), lambda i: (0, 0)),
            pl.BlockSpec((1, tokens, step), lambda i: (i, 0, 0)),
        ],
        out_specs=[spec, spec],
        out_shape=[jax.ShapeDtypeStruct(half + (3 * step,), BF)] * 2,
        compiler_params=PARAMS,
    )(own, rows_t, parts)


def input_kernel(*refs):
    base_ref, weight_ref, pieces, out_ref = refs[0], refs[1], refs[2:-1], refs[-1]
    width = base_ref.shape[1]
    step = pieces[0].shape[2]
    total = base_ref[...]
    for i, ref in enumerate(pieces):
        for part in range(3):
            first = part * width + i * step
            total += contract_cols(ref[part], weight_ref[:, first : first + step])
    out_ref[...] = total.astype(BF)


def input_call(base, head, pieces):
    tokens, width = base.shape
    step = pieces[0].shape[2]
    row = pl.BlockSpec((TILE, width), lambda i: (i, 0))
    return pl.pallas_call(
        input_kernel,
        grid=(tokens // TILE,),
        name="input_grad",
        in_specs=[row, pl.BlockSpec(head.shape, lambda i: (0, 0))]
        + [pl.BlockSpec((3, TILE, step), lambda i: (0, i, 0))] * len(pieces),
        out_specs=row,
        out_shape=jax.ShapeDtypeStruct((tokens, width), BF),
        compiler_params=PARAMS,
    )(base, head, *pieces)


def swap(value, bit, devices):
    return lax.ppermute(value, AXES, [(i, i ^ (1 << bit)) for i in range(devices)])


def bit_orders(bits):
    rest = list(range(1, bits))
    starts = (0, (bits - 1) // 4, (bits - 1) // 2)
    return [[0] + rest[s:] + rest[:s] for s in starts]


def spans(width, parts):
    step = width // PAIR // parts * PAIR
    edges = [step * p for p in range(parts)] + [width]
    return list(zip(edges[:-1], edges[1:]))


class Chain:
    def __init__(self, value, order, devices, kind=BF, pair=None):
        self.devices, self.kind, self.order = devices, kind, list(order)
        self.left = list(range(devices.bit_length() - 1))
        self.bits = len(self.left)
        self.lead = value.shape[:-2]
        shape = self.lead + (2,) * self.bits + (value.shape[-2] // devices, value.shape[-1])
        self.got = None
        if pair is None:
            self.halve([value.reshape(shape)])
        else:
            self.left.pop()
            self.keep, self.send = (half.reshape(shape[1:]) for half in pair)

    def halve(self, terms):
        bit = self.order[0]
        axis = len(self.lead) + self.left.index(self.bits - 1 - bit)
        own = (lax.axis_index(AXES) >> bit) & 1
        mine = [lax.dynamic_index_in_dim(t, own, axis, keepdims=False) for t in terms]
        theirs = [lax.dynamic_index_in_dim(t, 1 - own, axis, keepdims=False) for t in terms]
        self.keep = mine[0] if len(terms) == 1 else mine[0].astype(F32) + mine[1].astype(F32)
        send = theirs[0] if len(terms) == 1 else theirs[0].astype(F32) + theirs[1].astype(F32)
        self.send = send.astype(self.kind)
        self.left.pop(axis - len(self.lead))

    def begin(self):
        self.got = swap(self.send, self.order.pop(0), self.devices)

    def finish(self):
        got, self.got = self.got, None
        if self.order:
            self.halve([self.keep, got])
        else:
            self.keep, self.send = self.keep.astype(F32) + got.astype(F32), None

    @property
    def over(self):
        return self.send is None


def tick(chains, value):
    active = [c for c in chains if not c.over]
    for c in active:
        if c.got is not None:
            c.finish()
    held = lax.optimization_barrier((value, [(c.keep, c.send) for c in active]))
    for c, (keep, send) in zip(active, held[1]):
        c.keep, c.send = keep, send
        if not c.over:
            c.begin()
    return held[0]


def chains_of(value, devices, parts=3, turn=0, kind=BF):
    orders = bit_orders(devices.bit_length() - 1)
    return [
        Chain(value[:, a:b], orders[(p + turn) % 3], devices, kind)
        for p, (a, b) in enumerate(spans(value.shape[1], parts))
    ]


def result(chains):
    return jnp.concatenate([c.keep for c in chains], axis=1)


def join(halves, axis):
    mine, got = halves
    own = lax.axis_index(AXES) & 1
    return jnp.where(own == 0, jnp.stack([mine, got], axis), jnp.stack([got, mine], axis))


def gather_halves(values, devices, later):
    bits = devices.bit_length() - 1
    here = lax.axis_index(AXES)
    orders = [order[::-1] for order in bit_orders(bits)]
    orders = [orders[p % 3] for p in range(len(values))]
    work = list(values)
    held = [[] for _ in values]
    for step in range(bits - 1):
        for p in range(len(work)):
            bit = orders[p][step]
            name = bits - 1 - bit
            axis = sum(1 for h in held[p] if h < name)
            own = (here >> bit) & 1
            mine, got = work[p], swap(work[p], bit, devices)
            work[p] = jnp.where(own == 0, jnp.stack([mine, got], axis), jnp.stack([got, mine], axis))
            held[p] = sorted(held[p] + [name])
        if step == bits - 4:
            work, later = lax.optimization_barrier((work, later))
    work = [w.reshape(devices // 2, *v.shape) for w, v in zip(work, values)]
    return [(w, swap(w, 0, devices)) for w in work], later


def widen(vector):
    return vector.astype(F32)


def local(
    tokens, segment_ids, cotangent, w_query, b_query, w_key, w_value, b_value, w_out, b_out,
    gain_attn, shift_attn, w_up, b_up, w_down, b_down, gain_ffn, shift_ffn, devices,
):
    blocks, length, width = tokens.shape
    rows = tokens.reshape(blocks * length, width)
    rows_t = turned(rows)
    own = w_query.shape[0]
    ratio = b_up.shape[0] // own
    vectors = [b_query, b_value, b_out, gain_attn, shift_attn, b_down, gain_ffn, shift_ffn]
    names = len(vectors)
    side = jnp.stack(vectors, axis=1)
    side = jnp.concatenate([side, b_up.reshape(own, ratio)], axis=1)
    side = jnp.pad(side, ((0, 0), (0, PAIR - names - ratio)))
    down_side = w_down.reshape(ratio, own, width).transpose(1, 0, 2).reshape(own, ratio * width)
    later = jnp.concatenate([down_side, w_up, w_out], axis=1).astype(BF)
    values = [v.astype(BF) for v in (w_query, w_key, w_value, side)]
    halves, (later, rows_t) = gather_halves(values, devices, (later, rows_t))
    head = join(halves.pop(), 1).reshape(devices * own, PAIR)
    query_bias, value_bias, out_bias, attn_gain, attn_shift, down_bias, ffn_gain, ffn_shift = [
        widen(head[:, i]) for i in range(names)
    ]
    up_bias = widen(head[:, names : names + ratio].reshape(-1))
    rest = lax.all_gather(later, AXES, axis=0, tiled=True)
    units = ratio * width
    up_full, out_full = rest[:, units : 2 * units], rest[:, 2 * units :]
    down_rows, own_rows = rest, own
    if own % 32:
        own_rows = 32
        down_rows = rest[:, :units].reshape(devices, own, ratio, width).transpose(0, 2, 1, 3)
        down_rows = down_rows.reshape(-1, ratio, own_rows, width).transpose(0, 2, 1, 3).reshape(width, units)

    packed_bias = jnp.concatenate([query_bias, jnp.zeros_like(query_bias), value_bias])
    if own % 32 == 0:
        packed, packed_full = project(rows, halves, packed_bias)
    else:
        packed_full = jnp.concatenate([join(pair, 1).reshape(width, -1) for pair in halves], axis=1)
        packed = (matmul(rows, packed_full) + packed_bias).astype(BF)
    segments = segment_ids.reshape(-1)
    context, logsums = attend(segments, packed)
    attended = matmul(context, out_full) + out_bias
    first, normed_one, inverse_one = normalize(rows.astype(F32) + attended, attn_gain, attn_shift)
    first_low = first.astype(BF)
    hidden, slope = up_call(first_low, rest, up_bias)
    output, grad_two, grad_branch, ffn_gain_grad, ffn_shift_grad, down_bias_grad = settle(
        hidden, down_rows, down_bias, first, ffn_gain, ffn_shift,
        cotangent.reshape(blocks * length, width), own_rows,
    )
    encoder_output = output.reshape(tokens.shape)
    ffn_gain_grad, ffn_shift_grad, down_bias_grad = ffn_gain_grad[0], ffn_shift_grad[0], down_bias_grad[0]

    down = chains_of(contract_rows(hidden, grad_branch).astype(BF), devices, parts=2)
    running = list(down)
    grad_branch = tick(running, grad_branch)
    grad_pre, up_bias_grad = up_back_call(grad_branch, down_rows, slope, own_rows)
    up_bias_grad = up_bias_grad[0]
    grad_pre = tick(running, grad_pre)
    up_product = contract_rows(first_low, grad_pre).astype(BF)
    up = chains_of(up_product, devices, parts=2, turn=2)
    running += up
    grad_pre = tick(running, grad_pre)
    grad_first = grad_two + contract_cols(grad_pre, up_full)
    grad_one, attn_gain_grad, attn_shift_grad = normalize_back(
        grad_first, normed_one, inverse_one, attn_gain
    )
    grad_attended = grad_one.astype(BF)
    out_bias_grad = jnp.sum(grad_attended.astype(F32), axis=0)
    out_product = contract_rows(context, grad_attended).astype(BF)
    out = chains_of(out_product, devices, parts=1, turn=2)
    grad_context = contract_cols(grad_attended, out_full).astype(BF)
    running += out

    pieces, shares = [], []
    for chunk in range(CHUNKS):
        grad_context = tick(running, grad_context)
        piece = attend_back(segments, packed, grad_context, logsums, chunk)
        if chunk + 1 < CHUNKS:
            grad_context, piece = lax.optimization_barrier((grad_context, piece))
        pieces.append(piece)
        if own % 32 == 0:
            pair = weight_halves(rows_t, piece[0], devices)
            order = bit_orders(devices.bit_length() - 1)[chunk % 3]
            grads = jax.ShapeDtypeStruct((width, pair[0].shape[2]), BF)
            shares.append([Chain(grads, order, devices, pair=pair)])
        else:
            grads = jnp.concatenate([matmul(rows_t, piece[0][part]).astype(BF) for part in range(3)], axis=1)
            shares.append(chains_of(grads, devices, parts=1, turn=chunk))
        running += shares[-1]
    joined = [jnp.concatenate([piece[part] for piece in pieces], axis=1) for part in (1, 2)]
    vector_grads = [
        joined[0][0], joined[1][0], out_bias_grad, attn_gain_grad, attn_shift_grad,
        down_bias_grad, ffn_gain_grad, ffn_shift_grad,
    ]
    side_grad = jnp.concatenate(
        [v.reshape(devices, own) for v in vector_grads] + [up_bias_grad.reshape(devices, own * ratio)],
        axis=1,
    )
    side = chains_of(side_grad, devices, parts=1, kind=F32)
    running += side
    tick(running, ())
    pieces = tick(running, [piece[0] for piece in pieces])
    total_input = input_call(grad_one, packed_full, pieces)
    layer_input_gradient = total_input.reshape(tokens.shape)
    while not all(c.over for c in running):
        tick(running, ())

    down_grad, up_grad, out_grad = result(down), result(up), result(out)
    shares = [result(share) for share in shares]
    step = width // CHUNKS
    query_grad, key_grad, value_grad = [
        jnp.concatenate([share[:, part * step : (part + 1) * step] for share in shares], axis=1)
        for part in range(3)
    ]
    side_grad = result(side)[0]
    parts = [side_grad[i * own : (i + 1) * own] for i in range(names)]
    up_bias_share = side_grad[names * own :]
    return (
        encoder_output, layer_input_gradient, query_grad, parts[0], key_grad, value_grad, parts[1],
        out_grad, parts[2], parts[3], parts[4], up_grad, up_bias_share, down_grad, parts[5],
        parts[6], parts[7],
    )


def solution(mesh):
    devices = mesh.shape["fsdp"] * mesh.shape["rep"]
    act, ids = P("rep", "fsdp", None), P("rep", "fsdp")
    mat, vec = P(AXES, None), P(AXES)
    return jax.shard_map(
        partial(local, devices=devices),
        mesh=mesh,
        in_specs=(
            act, ids, act, mat, vec, mat, mat, vec, mat, vec, vec, vec, mat, vec, mat, vec, vec, vec,
        ),
        out_specs=(act, act, mat, vec, mat, mat, vec, mat, vec, vec, vec, mat, vec, mat, vec, vec, vec),
        check_vma=False,
    )
```
